32 devices in a mesh: rows: 2 (over y), seq: 16 (over z, x, core).
Axes of the slice: x: 2, y: 2, z: 4, core: 2. Of those that a mesh axis runs over, the one named last changes fastest.
Arguments:
- tokens: bfloat16 [2, 2048, 2304], P('rows', 'seq'), may hold values from -6 to 6
- cotangent: bfloat16 [2, 2048, 2304], P('rows', 'seq'), may hold values from -6 to 6
- doc_ids: int32 [2, 2048], P('rows'), may hold values from 0 to 3, as said below
- bit_levels: int32 [7], replicated, may hold values from 0 to 2, as said below
- w_query: int32 [2304, 2048], P(('rows', 'seq')), may hold values from -128 to 127
- w_key: int32 [2304, 1024], P(('rows', 'seq')), may hold values from -128 to 127
- w_value: int32 [2304, 1024], P(('rows', 'seq')), may hold values from -128 to 127
- w_proj: int32 [2304, 2048], P(('rows', 'seq')), may hold values from -128 to 127
- w_gate: int32 [2304, 9216], P(('rows', 'seq')), may hold values from -128 to 127
- w_up: int32 [2304, 9216], P(('rows', 'seq')), may hold values from -128 to 127
- w_down: int32 [2304, 9216], P(('rows', 'seq')), may hold values from -128 to 127
- gain_first: float32 [2304], replicated, may hold values from -0.5 to 0.5
- gain_second: float32 [2304], replicated, may hold values from -0.5 to 0.5
- gain_third: float32 [2304], replicated, may hold values from -0.5 to 0.5
- gain_fourth: float32 [2304], replicated, may hold values from -0.5 to 0.5
Outputs:
- layer_out: bfloat16 [2, 2048, 2304], P('rows', 'seq')
- grad_tokens: float32 [2, 2048, 2304], P('rows', 'seq')
- grad_query: float32 [2304, 2048], P(('rows', 'seq'))
- grad_key: float32 [2304, 1024], P(('rows', 'seq'))
- grad_value: float32 [2304, 1024], P(('rows', 'seq'))
- grad_proj: float32 [2304, 2048], P(('rows', 'seq'))
- grad_gate: float32 [2304, 9216], P(('rows', 'seq'))
- grad_up: float32 [2304, 9216], P(('rows', 'seq'))
- grad_down: float32 [2304, 9216], P(('rows', 'seq'))
- grad_first: float32 [2304], P(('rows', 'seq'))
- grad_second: float32 [2304], P(('rows', 'seq'))
- grad_third: float32 [2304], P(('rows', 'seq'))
- grad_fourth: float32 [2304], P(('rows', 'seq'))
The draws below stay inside these ranges and needn't reach their ends.
Inputs may be any that keep to these rules, and one draw needn't show every extreme that they name: `doc_ids`: ids never fall along a row. Rows of even index hold one document (id 0); rows of odd index hold up to four, and their last token has id 3. `bit_levels`: level 0 occurs three times, levels 1 and 2 twice each.
All inputs are finite; a program needn't handle non-finite values.
Results may differ from the reference program's by a relative error of at most 0.019.
The reference program's roundings to bfloat16 on the way count: a program that leaves them out, or rounds other values in their place, can miss the bound.
Values may be sent and summed in bfloat16 or wider, within the bound.
A program may use at most 448 MiB of HBM per device.

```python
import math
from functools import partial
import jax
import jax.numpy as jnp
from jax import lax

D = 2304
FF = 9216
HEADS = 8
KV_HEADS = 4
HEAD_DIM = 256
ROW_LEN = 2048
ROWS = 2


def draw_doc_ids(key, part):
    cuts = jax.random.randint(key, (ROWS, 3), 1, ROW_LEN)
    places = jnp.arange(ROW_LEN, dtype=jnp.int32)
    counted = jnp.sum((places[None, :, None] >= cuts[:, None, :]).astype(jnp.int32), axis=2)
    packed = (jnp.arange(ROWS, dtype=jnp.int32) % 2)[:, None]
    return (counted * packed).astype(jnp.int32)


def draw_bit_levels(key, part):
    return (jax.random.permutation(key, 7) % 3).astype(jnp.int32)


def place_ends(values, rng, smallest, top_value):
    longest = values.shape.index(max(values.shape))
    spots = []
    for shift in (0, 1):
        where = [jax.random.randint(jax.random.fold_in(rng, axis), (), 0, length) for axis, length in enumerate(values.shape)]
        where[longest] = (where[longest] + shift) % values.shape[longest]
        spots.append(tuple(where))
    return values.at[spots[0]].set(smallest).at[spots[1]].set(top_value)


def levels(own_key, extent, cuts, least, high):
    loudness = 1.0
    for position, shards_of in cuts:
        heights = jax.random.uniform(jax.random.fold_in(jax.random.fold_in(own_key, 6), position), (shards_of,), jnp.float32, least / len(cuts), high / len(cuts))
        loudness = loudness * jnp.repeat(jnp.exp(heights), extent[position] // shards_of).reshape((-1,) + (1,) * (len(extent) - 1 - position))
    return loudness


def normal_values(key, extent, deviation, reach, pieces=(), held_as=jnp.bfloat16):
    values = deviation * jax.random.normal(key, extent, jnp.float32)
    if pieces:
        values = values * levels(key, extent, pieces, -0.22, 0.18)
    return jnp.clip(values, -reach, reach).astype(held_as)


def setup_inputs(seed: int = 0) -> dict:
    key_list = jax.random.split(jax.random.key(seed), 16)
    return {
        "tokens": normal_values(key_list[0], (ROWS, ROW_LEN, D), 1.0, 6.0, ((0, 2), (1, 16))),
        "cotangent": normal_values(key_list[1], (ROWS, ROW_LEN, D), 1.0, 6.0, ((0, 2), (1, 16))),
        "doc_ids": draw_doc_ids(jax.random.fold_in(key_list[15], 71), 0),
        "bit_levels": draw_bit_levels(jax.random.fold_in(key_list[15], 71), 0),
        "w_query": place_ends(jax.random.randint(key_list[4], (D, HEADS * HEAD_DIM), -128, 128), jax.random.fold_in(key_list[4], 1), -128, 127).astype(jnp.int32),
        "w_key": place_ends(jax.random.randint(key_list[5], (D, KV_HEADS * HEAD_DIM), -128, 128), jax.random.fold_in(key_list[5], 1), -128, 127).astype(jnp.int32),
        "w_value": place_ends(jax.random.randint(key_list[6], (D, KV_HEADS * HEAD_DIM), -128, 128), jax.random.fold_in(key_list[6], 1), -128, 127).astype(jnp.int32),
        "w_proj": place_ends(jax.random.randint(key_list[7], (D, HEADS * HEAD_DIM), -128, 128), jax.random.fold_in(key_list[7], 1), -128, 127).astype(jnp.int32),
        "w_gate": place_ends(jax.random.randint(key_list[8], (D, FF), -128, 128), jax.random.fold_in(key_list[8], 1), -128, 127).astype(jnp.int32),
        "w_up": place_ends(jax.random.randint(key_list[9], (D, FF), -128, 128), jax.random.fold_in(key_list[9], 1), -128, 127).astype(jnp.int32),
        "w_down": place_ends(jax.random.randint(key_list[10], (D, FF), -128, 128), jax.random.fold_in(key_list[10], 1), -128, 127).astype(jnp.int32),
        "gain_first": jnp.clip(jax.random.uniform(key_list[11], (D,), jnp.float32, -0.5, 0.5), -0.5, 0.5),
        "gain_second": jnp.clip(jax.random.uniform(key_list[12], (D,), jnp.float32, -0.5, 0.5), -0.5, 0.5),
        "gain_third": jnp.clip(jax.random.uniform(key_list[13], (D,), jnp.float32, -0.5, 0.5), -0.5, 0.5),
        "gain_fourth": jnp.clip(jax.random.uniform(key_list[14], (D,), jnp.float32, -0.5, 0.5), -0.5, 0.5),
    }


@jax.custom_vjp
def low(v):
    return lax.optimization_barrier(v.astype(jnp.bfloat16)).astype(jnp.float32)

@jax.custom_vjp
def low_back(v):
    return v

def low_keep(v):
    return (low(v), None)

def low_pass(kept, grad):
    return (grad,)

def back_keep(v):
    return (v, None)

def back_low(kept, grad):
    return (low(grad),)
low.defvjp(low_keep, low_pass)
low_back.defvjp(back_keep, back_low)
highest = lax.Precision.HIGHEST
softcap = 50.0
epsilon = 1e-06
qk_boost = 1.65

def dequant(levels_int, level_idx, fan_in, boost):
    stride = jnp.where(level_idx == 0, 1, jnp.where(level_idx == 1, 16, 64)).astype(jnp.int32)
    sliced = levels_int // stride * stride + stride // 2
    return sliced.astype(jnp.float32) * (boost / (74.0 * math.sqrt(fan_in)))

def rmsnorm(values, gain_vec):
    return values * lax.rsqrt(lax.optimization_barrier(jnp.mean(values * values, axis=-1, keepdims=True)) + epsilon) * (1.0 + gain_vec)

def rotate(values, positions, direction):
    half_dim = HEAD_DIM // 2
    frequency = 10000.0 ** (-(2.0 / HEAD_DIM) * jnp.arange(half_dim, dtype=jnp.float32))
    angles = positions.astype(jnp.float32)[:, None] * frequency[None, :]
    cosine = jnp.cos(angles)[:, None, :]
    sine = jnp.sin(angles)[:, None, :] * direction
    front_half = values[..., :half_dim]
    back_half = values[..., half_dim:]
    return jnp.concatenate([front_half * cosine - back_half * sine, back_half * cosine + front_half * sine], axis=-1)

def product(left_side, right_side):
    return jnp.dot(left_side, right_side, precision=highest)

def product_t(left_side, right_side):
    return jnp.dot(left_side, right_side.T, precision=highest)

def attend_row(row_inputs):
    query_row, key_row, value_row, docs_row = row_inputs
    length = key_row.shape[0]
    query_block = min(512, length)
    group_size = HEADS // KV_HEADS
    key_wide = jnp.repeat(key_row, group_size, axis=1)
    value_wide = jnp.repeat(value_row, group_size, axis=1)
    key_pos = jnp.arange(length, dtype=jnp.int32)

    def attend_pair(paired):
        query_part, first_row = paired
        raw_scores = low_back(jnp.einsum('qhd,khd->hqk', query_part, key_wide, precision=highest) * HEAD_DIM ** (-0.5))
        capped = softcap * jnp.tanh(raw_scores / softcap)
        query_pos = first_row + jnp.arange(query_block, dtype=jnp.int32)
        query_docs = lax.dynamic_slice_in_dim(docs_row, first_row, query_block)
        allowed = (key_pos[None, :] <= query_pos[:, None]) & (docs_row[None, :] == query_docs[:, None])
        weights = jnp.where(allowed[None], jnp.exp(capped), 0.0)
        totals = lax.optimization_barrier(jnp.sum(weights, axis=-1))
        summed = low_back(jnp.einsum('hqk,khd->qhd', low(weights), value_wide, precision=highest))
        return summed / jnp.transpose(totals)[:, :, None]
    blocks = length // query_block
    query_parts = query_row.reshape(blocks, query_block, HEADS, HEAD_DIM)
    starts = jnp.arange(blocks, dtype=jnp.int32) * query_block
    mixed = lax.map(jax.checkpoint(attend_pair), (query_parts, starts))
    return mixed.reshape(length, HEADS, HEAD_DIM)

def forward(tokens_f, query_w, key_w, value_w, proj_w, gate_w, up_w, down_w, gain_first, gain_second, gain_third, gain_fourth, doc_ids):
    rows_all = tokens_f.shape[0]
    length = tokens_f.shape[1]
    flat_tokens = tokens_f.reshape(rows_all * length, D)
    normed_in = low(rmsnorm(flat_tokens, gain_first))
    query_pre = low_back(product(normed_in, low(query_w)))
    key_pre = low_back(product(normed_in, low(key_w)))
    value_all = low(low_back(product(normed_in, low(value_w)))).reshape(rows_all, length, KV_HEADS, HEAD_DIM)
    positions = jnp.arange(length, dtype=jnp.int32)
    query_rot = low(rotate(query_pre.reshape(rows_all, length, HEADS, HEAD_DIM), positions, 1.0))
    key_rot = low(rotate(key_pre.reshape(rows_all, length, KV_HEADS, HEAD_DIM), positions, 1.0))
    mixed = lax.map(attend_row, (query_rot, key_rot, value_all, doc_ids))
    mixed_low = low(mixed.reshape(rows_all * length, HEADS * HEAD_DIM))
    attn_out = low_back(product_t(mixed_low, low(proj_w)))
    hidden_one = flat_tokens + rmsnorm(attn_out, gain_second)
    normed_mid = low(rmsnorm(hidden_one, gain_third))
    gate_pre = low_back(product(normed_mid, low(gate_w)))
    up_pre = low_back(product(normed_mid, low(up_w)))
    activated = low(jax.nn.gelu(gate_pre, approximate=True) * up_pre)
    ffn_out = low_back(product_t(activated, low(down_w)))
    result = hidden_one + rmsnorm(ffn_out, gain_fourth)
    return result.reshape(rows_all, length, D)

def reference(tokens, cotangent, doc_ids, bit_levels, w_query, w_key, w_value, w_proj, w_gate, w_up, w_down, gain_first, gain_second, gain_third, gain_fourth):
    attn_fan = HEADS * HEAD_DIM
    layer_f, pullback = jax.vjp(partial(forward, doc_ids=doc_ids), tokens.astype(jnp.float32), dequant(w_query, bit_levels[0], D, qk_boost), dequant(w_key, bit_levels[1], D, qk_boost), dequant(w_value, bit_levels[2], D, 1.0), dequant(w_proj, bit_levels[3], attn_fan, 1.0), dequant(w_gate, bit_levels[4], D, 1.0), dequant(w_up, bit_levels[5], D, 1.0), dequant(w_down, bit_levels[6], FF, 1.0), gain_first, gain_second, gain_third, gain_fourth)
    grads = pullback(cotangent.astype(jnp.float32))
    return (layer_f.astype(jnp.bfloat16), grads[0], grads[1], grads[2], grads[3], grads[4], grads[5], grads[6], grads[7], grads[8], grads[9], grads[10], grads[11])
```

```python
import math

import jax
import jax.numpy as jnp
from jax import lax
from jax.sharding import PartitionSpec as P

D = 2304
FF = 9216
HEADS = 8
KV_HEADS = 4
HEAD_DIM = 256


softcap = 50.0
epsilon = 1e-06
qk_boost = 1.65


def dequant(levels_int, level_idx, fan_in, boost):
    bits = jnp.where(level_idx == 0, 0, jnp.where(level_idx == 1, 4, 6)).astype(jnp.int32)
    middle = jnp.where(level_idx == 0, 0, jnp.where(level_idx == 1, 8, 32)).astype(jnp.int32)
    sliced = ((levels_int >> bits) << bits) + middle
    return sliced.astype(jnp.float32) * (boost / (74.0 * math.sqrt(fan_in)))


def rmsnorm(values, gain_vec):
    return (
        values
        * lax.rsqrt(jnp.mean(values * values, axis=-1, keepdims=True) + epsilon)
        * (1.0 + gain_vec)
    )


def rotate(values, positions, direction):
    half_dim = HEAD_DIM // 2
    frequency = 10000.0 ** (-(2.0 / HEAD_DIM) * jnp.arange(half_dim, dtype=jnp.float32))
    angles = positions.astype(jnp.float32)[:, None] * frequency[None, :]
    cosine = jnp.cos(angles)[:, None, :]
    sine = jnp.sin(angles)[:, None, :] * direction
    front_half = values[..., :half_dim]
    back_half = values[..., half_dim:]
    return jnp.concatenate(
        [front_half * cosine - back_half * sine, back_half * cosine + front_half * sine], axis=-1
    )


def gelu_product(gate_vals, up_vals):
    return jax.nn.gelu(gate_vals, approximate=True) * up_vals


def per_device_plain(
    tokens,
    cotangent,
    doc_ids,
    bit_levels,
    w_query,
    w_key,
    w_value,
    w_proj,
    w_gate,
    w_up,
    w_down,
    gain_first,
    gain_second,
    gain_third,
    gain_fourth,
):
    rows_here = tokens.shape[0]
    seq_block = tokens.shape[1]
    token_count = rows_here * seq_block
    local_rows = w_query.shape[0]
    group_size = HEADS // KV_HEADS
    query_width = HEADS * HEAD_DIM
    key_width = KV_HEADS * HEAD_DIM
    score_scale = HEAD_DIM ** (-0.5)
    offset = lax.axis_index("seq") * seq_block
    positions = offset + jnp.arange(seq_block, dtype=jnp.int32)
    query_docs = lax.dynamic_slice_in_dim(doc_ids, offset, seq_block, 1)
    query_local = dequant(w_query, bit_levels[0], D, qk_boost).astype(jnp.bfloat16)
    key_local = dequant(w_key, bit_levels[1], D, qk_boost).astype(jnp.bfloat16)
    value_local = dequant(w_value, bit_levels[2], D, 1.0).astype(jnp.bfloat16)
    proj_local = dequant(w_proj, bit_levels[3], query_width, 1.0).astype(jnp.bfloat16)
    gate_local = dequant(w_gate, bit_levels[4], D, 1.0).astype(jnp.bfloat16)
    up_local = dequant(w_up, bit_levels[5], D, 1.0).astype(jnp.bfloat16)
    down_local = dequant(w_down, bit_levels[6], FF, 1.0).astype(jnp.bfloat16)
    query_full, key_full, value_full, proj_full = (
        lax.all_gather(query_local, ("rows", "seq"), axis=0, tiled=True),
        lax.all_gather(key_local, ("rows", "seq"), axis=0, tiled=True),
        lax.all_gather(value_local, ("rows", "seq"), axis=0, tiled=True),
        lax.all_gather(proj_local, ("rows", "seq"), axis=0, tiled=True),
    )
    row_groups = lax.axis_size("rows")
    seq_count = lax.axis_size("seq")
    col_width = FF // seq_count
    stacked = jnp.stack([gate_local, up_local, down_local]).reshape(
        3, local_rows, seq_count, col_width
    )
    spread = jnp.concatenate([stacked] * row_groups, axis=2)
    columns_all = lax.all_to_all(
        spread, ("rows", "seq"), split_axis=2, concat_axis=1, tiled=True
    ).reshape(3, D, col_width)
    gate_cols = columns_all[0]
    up_cols = columns_all[1]
    down_cols = columns_all[2]
    flat_tokens = tokens.astype(jnp.float32).reshape(token_count, D)
    normed_low = rmsnorm(flat_tokens, gain_first).astype(jnp.bfloat16)
    query_pre = jnp.dot(normed_low, query_full, preferred_element_type=jnp.float32)
    key_pre = jnp.dot(normed_low, key_full, preferred_element_type=jnp.float32)
    value_low = (
        jnp.dot(normed_low, value_full, preferred_element_type=jnp.float32)
        .astype(jnp.bfloat16)
        .reshape(rows_here, seq_block, KV_HEADS, HEAD_DIM)
    )
    query_rot = (
        rotate(query_pre.reshape(rows_here, seq_block, HEADS, HEAD_DIM), positions, 1.0)
        .astype(jnp.bfloat16)
        .reshape(rows_here, seq_block, KV_HEADS, group_size, HEAD_DIM)
    )
    key_rot = rotate(
        key_pre.reshape(rows_here, seq_block, KV_HEADS, HEAD_DIM), positions, 1.0
    ).astype(jnp.bfloat16)

    def piece_weights(key_piece):
        key_count = key_piece.shape[1]
        key_pos = jnp.arange(key_count, dtype=jnp.int32)
        raw_scores = (
            jnp.einsum(
                "bqgrd,bkgd->bgrqk", query_rot, key_piece, preferred_element_type=jnp.float32
            )
            * score_scale
        )
        allowed = (key_pos[None, :] <= positions[:, None])[None] & (
            doc_ids[:, None, :] == query_docs[:, :, None]
        )
        bent_score = jnp.tanh(raw_scores / softcap)
        weights = jnp.where(allowed[:, None, None], jnp.exp(softcap * bent_score), 0.0)
        return (weights, bent_score)

    key_piece = lax.all_gather(key_rot, "seq", axis=1, tiled=True)
    value_piece = lax.all_gather(value_low, "seq", axis=1, tiled=True)
    weights, bent_score = piece_weights(key_piece)
    summed = jnp.einsum(
        "bgrqk,bkgd->bqgrd",
        weights.astype(jnp.bfloat16),
        value_piece,
        preferred_element_type=jnp.float32,
    )
    totals, summed = (jnp.sum(weights, axis=-1), summed)
    denominator = jnp.transpose(totals, (0, 3, 1, 2))[..., None]
    mixed_out = summed / denominator
    mixed_low = mixed_out.astype(jnp.bfloat16).reshape(token_count, query_width)
    attn_out = jnp.einsum("th,dh->td", mixed_low, proj_full, preferred_element_type=jnp.float32)
    hidden_one = flat_tokens + rmsnorm(attn_out, gain_second)
    mid_low = rmsnorm(hidden_one, gain_third).astype(jnp.bfloat16)
    mid_row = lax.all_gather(mid_low.reshape(rows_here, seq_block, D), "seq", axis=1, tiled=True)
    gate_pre = jnp.einsum("btd,df->btf", mid_row, gate_cols, preferred_element_type=jnp.float32)
    up_pre = jnp.einsum("btd,df->btf", mid_row, up_cols, preferred_element_type=jnp.float32)
    activated = gelu_product(gate_pre, up_pre).astype(jnp.bfloat16)
    ffn_terms = jnp.einsum("btf,df->btd", activated, down_cols, preferred_element_type=jnp.float32)
    ffn_out = lax.psum_scatter(ffn_terms, "seq", scatter_dimension=1, tiled=True).reshape(
        token_count, D
    )
    result = hidden_one + rmsnorm(ffn_out, gain_fourth)
    layer_out = result.astype(jnp.bfloat16).reshape(rows_here, seq_block, D)
    upstream = cotangent.astype(jnp.float32).reshape(token_count, D)
    grad_ffn, fourth_part = jax.vjp(rmsnorm, ffn_out, gain_fourth)[1](upstream)
    grad_ffn_low = grad_ffn.astype(jnp.bfloat16)
    grad_row = lax.all_gather(
        grad_ffn_low.reshape(rows_here, seq_block, D), "seq", axis=1, tiled=True
    )
    grad_act = jnp.einsum("btd,df->btf", grad_row, down_cols, preferred_element_type=jnp.float32)
    grad_gate_pre, grad_up_pre = jax.vjp(gelu_product, gate_pre, up_pre)[1](grad_act)
    grad_gate_low = grad_gate_pre.astype(jnp.bfloat16)
    grad_up_low = grad_up_pre.astype(jnp.bfloat16)
    mid_terms = jnp.einsum(
        "btf,df->btd", grad_gate_low, gate_cols, preferred_element_type=jnp.float32
    ) + jnp.einsum("btf,df->btd", grad_up_low, up_cols, preferred_element_type=jnp.float32)
    grad_mid = lax.psum_scatter(mid_terms, "seq", scatter_dimension=1, tiled=True).reshape(
        token_count, D
    )
    column_terms = jnp.stack(
        [
            jnp.einsum("btd,btf->df", mid_row, grad_gate_low, preferred_element_type=jnp.float32),
            jnp.einsum("btd,btf->df", mid_row, grad_up_low, preferred_element_type=jnp.float32),
            jnp.einsum("btd,btf->df", grad_row, activated, preferred_element_type=jnp.float32),
        ]
    )
    returned = lax.all_to_all(
        column_terms.reshape(3, D, 1, col_width).astype(jnp.bfloat16),
        ("rows", "seq"),
        split_axis=1,
        concat_axis=2,
        tiled=True,
    ).astype(jnp.float32)
    column_sums = jnp.sum(
        returned.reshape(3, local_rows, row_groups, seq_count, col_width), axis=2
    ).reshape(3, local_rows, FF)
    hidden_part, third_part = jax.vjp(rmsnorm, hidden_one, gain_third)[1](grad_mid)
    grad_hidden = upstream + hidden_part
    grad_attn, second_part = jax.vjp(rmsnorm, attn_out, gain_second)[1](grad_hidden)
    grad_attn_low = grad_attn.astype(jnp.bfloat16)
    query_back, key_back, value_back, proj_back = (
        lax.all_gather(query_local, ("rows", "seq"), axis=0, tiled=True),
        lax.all_gather(key_local, ("rows", "seq"), axis=0, tiled=True),
        lax.all_gather(value_local, ("rows", "seq"), axis=0, tiled=True),
        lax.all_gather(proj_local, ("rows", "seq"), axis=0, tiled=True),
    )
    grad_mixed = jnp.dot(grad_attn_low, proj_back, preferred_element_type=jnp.float32).reshape(
        rows_here, seq_block, KV_HEADS, group_size, HEAD_DIM
    )
    grad_summed = (grad_mixed / denominator).astype(jnp.bfloat16)
    delta_rows = jnp.transpose(
        jnp.sum(grad_mixed * mixed_out, axis=-1) / denominator[..., 0], (0, 2, 3, 1)
    )
    key_piece = lax.all_gather(key_rot, "seq", axis=1, tiled=True)
    value_piece = lax.all_gather(value_low, "seq", axis=1, tiled=True)
    key_count = key_piece.shape[1]
    weights, bent_score = piece_weights(key_piece)
    grad_weights = (
        jnp.einsum(
            "bqgrd,bkgd->bgrqk", grad_summed, value_piece, preferred_element_type=jnp.float32
        )
        - delta_rows[..., None]
    )
    grad_raw = (weights * grad_weights * (1.0 - bent_score * bent_score)).astype(jnp.bfloat16)
    grad_queries = (
        jnp.einsum("bgrqk,bkgd->bqgrd", grad_raw, key_piece, preferred_element_type=jnp.float32)
        * score_scale
    )
    key_term = (
        jnp.einsum("bgrqk,bqgrd->bkgd", grad_raw, query_rot, preferred_element_type=jnp.float32)
        * score_scale
    )
    value_term = jnp.einsum(
        "bgrqk,bqgrd->bkgd",
        weights.astype(jnp.bfloat16),
        grad_summed,
        preferred_element_type=jnp.float32,
    )
    key_sums = key_term
    value_sums = value_term
    grad_query_rot, key_sums, value_sums = (grad_queries, key_sums, value_sums)
    grad_key_rot, grad_value_sum = (
        lax.psum_scatter(key_sums, "seq", scatter_dimension=1, tiled=True),
        lax.psum_scatter(value_sums, "seq", scatter_dimension=1, tiled=True),
    )
    grad_query_pre = (
        rotate(grad_query_rot.reshape(rows_here, seq_block, HEADS, HEAD_DIM), positions, -1.0)
        .astype(jnp.bfloat16)
        .reshape(token_count, query_width)
    )
    grad_key_pre = (
        rotate(grad_key_rot, positions, -1.0).astype(jnp.bfloat16).reshape(token_count, key_width)
    )
    grad_value_low = grad_value_sum.astype(jnp.bfloat16).reshape(token_count, key_width)
    grad_in = (
        jnp.einsum("tf,df->td", grad_query_pre, query_back, preferred_element_type=jnp.float32)
        + jnp.einsum("tf,df->td", grad_key_pre, key_back, preferred_element_type=jnp.float32)
        + jnp.einsum("tf,df->td", grad_value_low, value_back, preferred_element_type=jnp.float32)
    )
    tokens_part, first_part = jax.vjp(rmsnorm, flat_tokens, gain_first)[1](grad_in)
    grad_tokens = (grad_hidden + tokens_part).reshape(rows_here, seq_block, D)

    def outer_sum(left_side, right_side):
        return jnp.einsum("td,tf->df", left_side, right_side, preferred_element_type=jnp.float32)

    gain_terms = jnp.stack([first_part, second_part, third_part, fourth_part], axis=1)
    padding = jnp.zeros((D, 124), jnp.float32)
    weight_terms = jnp.concatenate(
        [
            outer_sum(normed_low, grad_query_pre),
            outer_sum(normed_low, grad_key_pre),
            outer_sum(normed_low, grad_value_low),
            outer_sum(grad_attn_low, mixed_low),
            gain_terms,
            padding,
        ],
        axis=1,
    )
    summed_terms = lax.psum_scatter(weight_terms, ("rows", "seq"), scatter_dimension=0, tiled=True)
    widths = [query_width, key_width, key_width, query_width]
    pieces_out = []
    column = 0
    for span_cols in widths:
        pieces_out.append(summed_terms[:, column : column + span_cols])
        column = column + span_cols
    return (
        layer_out,
        grad_tokens,
        pieces_out[0],
        pieces_out[1],
        pieces_out[2],
        pieces_out[3],
        column_sums[0],
        column_sums[1],
        column_sums[2],
        summed_terms[:, column],
        summed_terms[:, column + 1],
        summed_terms[:, column + 2],
        summed_terms[:, column + 3],
    )


AXES = ("rows", "seq")
LINE = 4


def moves(places, rule):
    found = []
    for index in range(places):
        y, rest = divmod(index, LINE * 4)
        z, x, c = rest // 4, (rest // 2) % 2, rest % 2
        target = rule(y, z, x, c)
        if target is not None:
            y_to, z_to, x_to, c_to = target
            found.append((index, y_to * LINE * 4 + (z_to * 2 + x_to) * 2 + c_to))
    return found


def send(value, rule):
    return lax.ppermute(value, AXES, moves(2 * LINE * 4, rule))


def to_row(value):
    return send(value, lambda y, z, x, c: (1 - y, z, x, c))


def to_x(value):
    return send(value, lambda y, z, x, c: (y, z, 1 - x, c))


def to_core(value):
    return send(value, lambda y, z, x, c: (y, z, x, 1 - c))


def to_pair(value):
    return send(value, lambda y, z, x, c: (y, z ^ 1, x, c))


def across_middle(value):
    return send(value, lambda y, z, x, c: (y, 3 - z, x, c) if z in (1, 2) else None)


def to_ends(value):
    return send(value, lambda y, z, x, c: (y, z ^ 1, x, c) if z in (1, 2) else None)


def from_ends(value):
    return send(value, lambda y, z, x, c: (y, z ^ 1, x, c) if z in (0, 3) else None)


def up_line(value):
    return send(value, lambda y, z, x, c: (y, z + 1, x, c) if z < LINE - 1 else None)


def down_line(value):
    return send(value, lambda y, z, x, c: (y, z - 1, x, c) if z > 0 else None)


def to_chip(value, dz, dx):
    return send(value, lambda y, z, x, c: (y, z ^ dz, x ^ dx, c))


def low(value):
    return value.astype(jnp.bfloat16)


def wide(value):
    return value.astype(jnp.float32)


def pick(array, index, axis=0):
    return lax.dynamic_index_in_dim(array, index, axis, keepdims=False)


def place(array, piece, starts):
    return lax.dynamic_update_slice(array, piece, starts)


class Spot:
    def __init__(self):
        self.y = lax.axis_index("rows")
        index = lax.axis_index("seq")
        self.z = index // 4
        self.x = (index // 2) % 2
        self.c = index % 2
        self.middle = (self.z == 1) | (self.z == 2)
        upper = self.z >= 2
        self.slots = [
            self.z,
            self.z ^ 1,
            jnp.where(upper, 1, 2).astype(jnp.int32),
            jnp.where(upper, 0, 3).astype(jnp.int32),
        ]


def gather_line(spot, own):
    pair = to_pair(own)
    near = across_middle(own)
    far = across_middle(pair)
    near_end = to_ends(near)
    far_end = to_ends(far)
    return [
        own,
        pair,
        jnp.where(spot.middle, near, near_end),
        jnp.where(spot.middle, far, far_end),
    ]


def reduce_line(parts):
    far = parts[3] + wide(from_ends(low(parts[3])))
    near = parts[2] + wide(from_ends(low(parts[2])))
    pair = parts[1] + wide(across_middle(low(far)))
    own = parts[0] + wide(across_middle(low(near)))
    return own + wide(to_pair(low(pair)))


def gather_group(own):
    over_x = to_x(own)
    return jnp.concatenate([own, to_core(own), over_x, to_core(over_x)], axis=0)


def reduce_group(parts):
    both = wide(parts[:, 0]) + wide(to_core(parts[:, 1]))
    return both[0] + wide(to_x(low(both[1])))


def gather_plane(spot, own):
    return [
        jnp.concatenate([block, to_x(block)], axis=0) for block in gather_line(spot, own)
    ]


def reduce_plane(chunks):
    parts = [None] * LINE
    for slot in (3, 2, 1, 0):
        parts[slot] = wide(chunks[slot][0]) + wide(to_x(chunks[slot][1]))
    return reduce_line(parts)


def member(spot, dx, dc):
    return (spot.x ^ dx) * 2 + (spot.c ^ dc)


def exchange_group(spot, pieces):
    own = pick(pieces, member(spot, 0, 0))
    from_core = to_core(pick(pieces, member(spot, 0, 1)))
    from_x = to_x(pick(pieces, member(spot, 1, 0)))
    from_both = to_core(to_x(pick(pieces, member(spot, 1, 1))))
    out = jnp.zeros_like(pieces)
    for dx, dc, piece in ((0, 0, own), (0, 1, from_core), (1, 0, from_x), (1, 1, from_both)):
        out = place(out, piece[None], (member(spot, dx, dc), 0, 0))
    return out


def gather_heads(spot, pieces):
    group = exchange_group(spot, pieces)
    rows, cols = pieces.shape[1:]
    out = jnp.zeros((2, LINE, 4, rows, cols), pieces.dtype)
    for slot, block in enumerate(gather_line(spot, group)):
        z = spot.slots[slot]
        out = place(out, block[None, None], (spot.y, z, 0, 0, 0))
        out = place(out, to_row(block)[None, None], (1 - spot.y, z, 0, 0, 0))
    return out.reshape(2 * LINE * 4 * rows, cols)


def scatter_heads(spot, sums):
    cols = sums.shape[1]
    rows = sums.shape[0] // (2 * LINE * 4)
    blocks = sums.reshape(2, LINE, 4, rows, cols)
    mine = pick(blocks, spot.y)
    other = pick(blocks, 1 - spot.y)
    parts = [None] * LINE
    for slot in (3, 2, 1, 0):
        z = spot.slots[slot]
        parts[slot] = wide(pick(mine, z)) + wide(to_row(pick(other, z)))
    return exchange_group(spot, low(reduce_line(parts)))


def gather_hidden(spot, pieces):
    rows, width = pieces.shape[1:]
    chip = spot.z * 2 + spot.x
    plane = jnp.zeros_like(pieces)
    for dz, dx in ((3, 0), (3, 1), (2, 0), (2, 1), (1, 0), (1, 1), (0, 1), (0, 0)):
        there = (spot.z ^ dz) * 2 + (spot.x ^ dx)
        piece = pick(pieces, there)
        if dz or dx:
            piece = to_chip(piece, dz, dx)
        plane = place(plane, piece[None], (there, 0, 0))
    across = to_row(plane)
    out = jnp.zeros((2, LINE * 2, 2, rows, width), pieces.dtype)
    for half, y in ((plane, spot.y), (across, 1 - spot.y)):
        out = place(out, half[None, :, None], (y, 0, spot.c, 0, 0))
        out = place(out, to_core(half)[None, :, None], (y, 0, 1 - spot.c, 0, 0))
    return out.reshape(2 * LINE * 4 * rows, width)


def scatter_hidden(spot, sums):
    width = sums.shape[1]
    rows = sums.shape[0] // (2 * LINE * 4)
    blocks = sums.reshape(2, LINE * 2, 2, rows, width)
    cores = low(
        wide(pick(blocks, spot.c, 2)) + wide(to_core(pick(blocks, 1 - spot.c, 2)))
    )
    plane = low(wide(pick(cores, spot.y)) + wide(to_row(pick(cores, 1 - spot.y))))
    out = jnp.zeros_like(plane)
    for dz, dx in ((3, 0), (3, 1), (2, 0), (2, 1), (1, 0), (1, 1), (0, 1), (0, 0)):
        there = (spot.z ^ dz) * 2 + (spot.x ^ dx)
        piece = pick(plane, there)
        if dz or dx:
            piece = to_chip(piece, dz, dx)
        out = place(out, piece[None], (there, 0, 0))
    return wide(out).transpose(1, 0, 2).reshape(rows, LINE * 2 * width)


def split_columns(matrix, count):
    rows, cols = matrix.shape
    return matrix.reshape(rows, count, cols // count).transpose(1, 0, 2)


def join_columns(blocks):
    count, rows, cols = blocks.shape
    return wide(blocks).transpose(1, 0, 2).reshape(rows, count * cols)


def turn(values, cosine, sine):
    half_dim = HEAD_DIM // 2
    front_half = values[..., :half_dim]
    back_half = values[..., half_dim:]
    return jnp.concatenate(
        [front_half * cosine - back_half * sine, back_half * cosine + front_half * sine], axis=-1
    )


def dot(left_side, right_side):
    return jnp.dot(left_side, right_side, preferred_element_type=jnp.float32)


def dot_rows(left_side, right_side):
    return jnp.einsum("tf,df->td", left_side, right_side, preferred_element_type=jnp.float32)


def outer_sum(left_side, right_side):
    return jnp.einsum("td,tf->df", left_side, right_side, preferred_element_type=jnp.float32)


def per_device_line(
    tokens,
    cotangent,
    doc_ids,
    bit_levels,
    w_query,
    w_key,
    w_value,
    w_proj,
    w_gate,
    w_up,
    w_down,
    gain_first,
    gain_second,
    gain_third,
    gain_fourth,
):
    spot = Spot()
    count = tokens.shape[1]
    local_rows = w_query.shape[0]
    group_size = HEADS // KV_HEADS
    query_width = HEADS * HEAD_DIM
    score_scale = HEAD_DIM ** (-0.5)
    span = 4 * count

    heads_in = low(
        jnp.concatenate(
            [
                split_columns(dequant(w_query, bit_levels[0], D, qk_boost), KV_HEADS),
                split_columns(dequant(w_key, bit_levels[1], D, qk_boost), KV_HEADS),
                split_columns(dequant(w_value, bit_levels[2], D, 1.0), KV_HEADS),
            ],
            axis=2,
        )
    )
    proj_in = low(split_columns(dequant(w_proj, bit_levels[3], query_width, 1.0), KV_HEADS))
    flat_tokens = wide(tokens).reshape(count, D)
    normed_low = low(rmsnorm(flat_tokens, gain_first))
    normed_all = gather_group(normed_low)
    heads_w = gather_heads(spot, heads_in)
    proj_w = gather_heads(spot, proj_in)
    chips = LINE * 2
    gate_w = gather_hidden(
        spot, low(split_columns(dequant(w_gate, bit_levels[4], D, 1.0), chips))
    )
    up_w = gather_hidden(spot, low(split_columns(dequant(w_up, bit_levels[5], D, 1.0), chips)))
    down_w = gather_hidden(
        spot, low(split_columns(dequant(w_down, bit_levels[6], FF, 1.0), chips))
    )

    inner = jnp.arange(count, dtype=jnp.int32)
    offsets = jnp.concatenate(
        [member(spot, dx, dc) * count + inner for dx in range(2) for dc in range(2)]
    )
    positions = spot.z * span + offsets
    half_dim = HEAD_DIM // 2
    frequency = 10000.0 ** (-(2.0 / HEAD_DIM) * jnp.arange(half_dim, dtype=jnp.float32))
    angles = positions.astype(jnp.float32)[:, None] * frequency[None, :]
    cosine = jnp.cos(angles)
    sine = jnp.sin(angles)
    docs = doc_ids.reshape(LINE, 2, 2, count)
    docs = jnp.where(spot.x == 1, docs[:, ::-1], docs)
    docs = jnp.where(spot.c == 1, docs[:, :, ::-1], docs).reshape(LINE, span)
    query_docs = pick(docs, spot.z)

    pre = dot(normed_all, heads_w)
    wide_q = group_size * HEAD_DIM
    query_rot = low(
        turn(
            pre[:, :wide_q].reshape(span, group_size, HEAD_DIM),
            cosine[:, None],
            sine[:, None],
        )
    )
    key_rot = low(turn(pre[:, wide_q : wide_q + HEAD_DIM], cosine, sine))
    value_low = low(pre[:, wide_q + HEAD_DIM :])
    key_value = [jnp.concatenate([key_rot, value_low], axis=1)]
    for _ in range(1, LINE):
        key_value.append(up_line(key_value[-1]))

    totals = 0.0
    summed = 0.0
    saved = []
    for back, block in enumerate(key_value):
        key_piece, value_piece = block[:, :HEAD_DIM], block[:, HEAD_DIM:]
        key_docs = pick(docs, jnp.maximum(spot.z - back, 0))
        key_pos = positions - back * span
        allowed = (
            (key_pos[None, :] <= positions[:, None])
            & (key_pos[None, :] >= 0)
            & (key_docs[None, :] == query_docs[:, None])
        )
        raw_scores = (
            jnp.einsum("qrd,kd->rqk", query_rot, key_piece, preferred_element_type=jnp.float32)
            * score_scale
        )
        bent = jnp.tanh(raw_scores / softcap)
        weights = jnp.where(allowed[None], jnp.exp(softcap * bent), 0.0)
        totals = totals + jnp.sum(weights, axis=-1)
        summed = summed + jnp.einsum(
            "rqk,kd->qrd", low(weights), value_piece, preferred_element_type=jnp.float32
        )
        saved.append((key_piece, value_piece, weights, bent))
    denominator = jnp.transpose(totals)[..., None]
    mixed_out = summed / denominator
    mixed_low = low(mixed_out).reshape(span, wide_q)
    attn_out = reduce_group(low(dot_rows(mixed_low, proj_w)).reshape(2, 2, count, D))
    hidden_one = flat_tokens + rmsnorm(attn_out, gain_second)
    mid_low = low(rmsnorm(hidden_one, gain_third))

    mid_chunks = gather_plane(spot, mid_low)
    gates, acts, ffn_chunks = [], [], []
    for chunk in mid_chunks:
        gate_pre = dot(chunk, gate_w)
        up_pre = dot(chunk, up_w)
        activated = low(gelu_product(gate_pre, up_pre))
        gates.append((gate_pre, up_pre))
        acts.append(activated)
        ffn_chunks.append(low(dot_rows(activated, down_w)).reshape(2, count, D))
    ffn_out = reduce_plane(ffn_chunks)
    result = hidden_one + rmsnorm(ffn_out, gain_fourth)
    layer_out = low(result).reshape(1, count, D)

    upstream = wide(cotangent).reshape(count, D)
    grad_ffn, fourth_part = jax.vjp(rmsnorm, ffn_out, gain_fourth)[1](upstream)
    grad_chunks = gather_plane(spot, low(grad_ffn))
    gate_grads, up_grads, back_chunks = [], [], []
    for chunk, (gate_pre, up_pre) in zip(grad_chunks, gates):
        grad_act = dot(chunk, down_w)
        grad_gate_pre, grad_up_pre = jax.vjp(gelu_product, gate_pre, up_pre)[1](grad_act)
        gate_grads.append(low(grad_gate_pre))
        up_grads.append(low(grad_up_pre))
        back_chunks.append(
            low(dot_rows(gate_grads[-1], gate_w) + dot_rows(up_grads[-1], up_w)).reshape(
                2, count, D
            )
        )
    grad_mid = reduce_plane(back_chunks)
    mid_all = jnp.concatenate(mid_chunks, axis=0)
    grad_gate = scatter_hidden(spot, low(outer_sum(mid_all, jnp.concatenate(gate_grads, axis=0))))
    grad_up = scatter_hidden(spot, low(outer_sum(mid_all, jnp.concatenate(up_grads, axis=0))))
    grad_down = scatter_hidden(
        spot,
        low(outer_sum(jnp.concatenate(grad_chunks, axis=0), jnp.concatenate(acts, axis=0))),
    )

    hidden_part, third_part = jax.vjp(rmsnorm, hidden_one, gain_third)[1](grad_mid)
    grad_hidden = upstream + hidden_part
    grad_attn, second_part = jax.vjp(rmsnorm, attn_out, gain_second)[1](grad_hidden)
    grad_attn_all = gather_group(low(grad_attn))
    proj_sums = scatter_heads(spot, low(outer_sum(grad_attn_all, mixed_low)))

    grad_mixed = dot(grad_attn_all, proj_w).reshape(span, group_size, HEAD_DIM)
    grad_summed = low(grad_mixed / denominator)
    delta = jnp.transpose(jnp.sum(grad_mixed * mixed_out, axis=-1)) / totals
    grad_query_rot = 0.0
    passed = None
    for back in range(LINE - 1, -1, -1):
        key_piece, value_piece, weights, bent = saved[back]
        grad_weights = (
            jnp.einsum(
                "qrd,kd->rqk", grad_summed, value_piece, preferred_element_type=jnp.float32
            )
            - delta[..., None]
        )
        grad_raw = low(weights * grad_weights * (1.0 - bent * bent))
        grad_query_rot = grad_query_rot + jnp.einsum(
            "rqk,kd->qrd", grad_raw, key_piece, preferred_element_type=jnp.float32
        )
        key_term = (
            jnp.einsum("rqk,qrd->kd", grad_raw, query_rot, preferred_element_type=jnp.float32)
            * score_scale
        )
        value_term = jnp.einsum(
            "rqk,qrd->kd", low(weights), grad_summed, preferred_element_type=jnp.float32
        )
        sums = jnp.concatenate([key_term, value_term], axis=1)
        if passed is not None:
            sums = sums + wide(down_line(passed))
        passed = low(sums)
    grad_query_pre = low(
        turn(grad_query_rot * score_scale, cosine[:, None], -sine[:, None])
    ).reshape(span, wide_q)
    grad_key_pre = low(turn(sums[:, :HEAD_DIM], cosine, -sine))
    grad_pre = jnp.concatenate([grad_query_pre, grad_key_pre, low(sums[:, HEAD_DIM:])], axis=1)
    head_sums = scatter_heads(spot, low(outer_sum(normed_all, grad_pre)))
    grad_in = reduce_group(low(dot_rows(grad_pre, heads_w)).reshape(2, 2, count, D))
    tokens_part, first_part = jax.vjp(rmsnorm, flat_tokens, gain_first)[1](grad_in)
    grad_tokens = (grad_hidden + tokens_part).reshape(1, count, D)

    gain_terms = lax.psum(jnp.stack([first_part, second_part, third_part, fourth_part]), AXES)
    mine = (spot.y * (LINE * 4) + lax.axis_index("seq")) * local_rows
    gains = lax.dynamic_slice_in_dim(gain_terms, mine, local_rows, 1)
    return (
        layer_out,
        grad_tokens,
        join_columns(head_sums[:, :, :wide_q]),
        join_columns(head_sums[:, :, wide_q : wide_q + HEAD_DIM]),
        join_columns(head_sums[:, :, wide_q + HEAD_DIM :]),
        join_columns(proj_sums),
        grad_gate,
        grad_up,
        grad_down,
        gains[0],
        gains[1],
        gains[2],
        gains[3],
    )


def solution(mesh):
    placed = (
        P("rows", "seq", None),
        P("rows", "seq", None),
        P("rows", None),
        P(),
        P(("rows", "seq"), None),
        P(("rows", "seq"), None),
        P(("rows", "seq"), None),
        P(("rows", "seq"), None),
        P(("rows", "seq"), None),
        P(("rows", "seq"), None),
        P(("rows", "seq"), None),
        P(),
        P(),
        P(),
        P(),
    )
    sizes = dict(mesh.shape)
    fits = sizes["rows"] == 2 and sizes["seq"] == LINE * 4
    return jax.shard_map(
        per_device_line if fits else per_device_plain,
        mesh=mesh,
        in_specs=placed,
        out_specs=(
            P("rows", "seq", None),
            P("rows", "seq", None),
            P(("rows", "seq"), None),
            P(("rows", "seq"), None),
            P(("rows", "seq"), None),
            P(("rows", "seq"), None),
            P(("rows", "seq"), None),
            P(("rows", "seq"), None),
            P(("rows", "seq"), None),
            P(("rows", "seq")),
            P(("rows", "seq")),
            P(("rows", "seq")),
            P(("rows", "seq")),
        ),
        check_vma=False,
    )
```

```python
import functools
import math

import jax
import jax.numpy as jnp
from jax import lax
from jax.experimental import pallas as pl
from jax.experimental.pallas import tpu as pltpu
from jax.sharding import PartitionSpec as P

D = 2304
FF = 9216
HEADS = 8
KV_HEADS = 4
HEAD_DIM = 256


softcap = 50.0
epsilon = 1e-06
qk_boost = 1.65


def dequant(levels_int, level_idx, fan_in, boost):
    bits = jnp.where(level_idx == 0, 0, jnp.where(level_idx == 1, 4, 6)).astype(jnp.int32)
    middle = jnp.where(level_idx == 0, 0, jnp.where(level_idx == 1, 8, 32)).astype(jnp.int32)
    sliced = ((levels_int >> bits) << bits) + middle
    return sliced.astype(jnp.float32) * (boost / (74.0 * math.sqrt(fan_in)))


def rmsnorm(values, gain_vec):
    return (
        values
        * lax.rsqrt(jnp.mean(values * values, axis=-1, keepdims=True) + epsilon)
        * (1.0 + gain_vec)
    )


def rotate(values, positions, direction):
    half_dim = HEAD_DIM // 2
    frequency = 10000.0 ** (-(2.0 / HEAD_DIM) * jnp.arange(half_dim, dtype=jnp.float32))
    angles = positions.astype(jnp.float32)[:, None] * frequency[None, :]
    cosine = jnp.cos(angles)[:, None, :]
    sine = jnp.sin(angles)[:, None, :] * direction
    front_half = values[..., :half_dim]
    back_half = values[..., half_dim:]
    return jnp.concatenate(
        [front_half * cosine - back_half * sine, back_half * cosine + front_half * sine], axis=-1
    )


def gelu_product(gate_vals, up_vals):
    return jax.nn.gelu(gate_vals, approximate=True) * up_vals


def per_device_plain(
    tokens,
    cotangent,
    doc_ids,
    bit_levels,
    w_query,
    w_key,
    w_value,
    w_proj,
    w_gate,
    w_up,
    w_down,
    gain_first,
    gain_second,
    gain_third,
    gain_fourth,
):
    rows_here = tokens.shape[0]
    seq_block = tokens.shape[1]
    token_count = rows_here * seq_block
    local_rows = w_query.shape[0]
    group_size = HEADS // KV_HEADS
    query_width = HEADS * HEAD_DIM
    key_width = KV_HEADS * HEAD_DIM
    score_scale = HEAD_DIM ** (-0.5)
    offset = lax.axis_index("seq") * seq_block
    positions = offset + jnp.arange(seq_block, dtype=jnp.int32)
    query_docs = lax.dynamic_slice_in_dim(doc_ids, offset, seq_block, 1)
    query_local = dequant(w_query, bit_levels[0], D, qk_boost).astype(jnp.bfloat16)
    key_local = dequant(w_key, bit_levels[1], D, qk_boost).astype(jnp.bfloat16)
    value_local = dequant(w_value, bit_levels[2], D, 1.0).astype(jnp.bfloat16)
    proj_local = dequant(w_proj, bit_levels[3], query_width, 1.0).astype(jnp.bfloat16)
    gate_local = dequant(w_gate, bit_levels[4], D, 1.0).astype(jnp.bfloat16)
    up_local = dequant(w_up, bit_levels[5], D, 1.0).astype(jnp.bfloat16)
    down_local = dequant(w_down, bit_levels[6], FF, 1.0).astype(jnp.bfloat16)
    query_full, key_full, value_full, proj_full = (
        lax.all_gather(query_local, ("rows", "seq"), axis=0, tiled=True),
        lax.all_gather(key_local, ("rows", "seq"), axis=0, tiled=True),
        lax.all_gather(value_local, ("rows", "seq"), axis=0, tiled=True),
        lax.all_gather(proj_local, ("rows", "seq"), axis=0, tiled=True),
    )
    row_groups = lax.axis_size("rows")
    seq_count = lax.axis_size("seq")
    col_width = FF // seq_count
    stacked = jnp.stack([gate_local, up_local, down_local]).reshape(
        3, local_rows, seq_count, col_width
    )
    spread = jnp.concatenate([stacked] * row_groups, axis=2)
    columns_all = lax.all_to_all(
        spread, ("rows", "seq"), split_axis=2, concat_axis=1, tiled=True
    ).reshape(3, D, col_width)
    gate_cols = columns_all[0]
    up_cols = columns_all[1]
    down_cols = columns_all[2]
    flat_tokens = tokens.astype(jnp.float32).reshape(token_count, D)
    normed_low = rmsnorm(flat_tokens, gain_first).astype(jnp.bfloat16)
    query_pre = jnp.dot(normed_low, query_full, preferred_element_type=jnp.float32)
    key_pre = jnp.dot(normed_low, key_full, preferred_element_type=jnp.float32)
    value_low = (
        jnp.dot(normed_low, value_full, preferred_element_type=jnp.float32)
        .astype(jnp.bfloat16)
        .reshape(rows_here, seq_block, KV_HEADS, HEAD_DIM)
    )
    query_rot = (
        rotate(query_pre.reshape(rows_here, seq_block, HEADS, HEAD_DIM), positions, 1.0)
        .astype(jnp.bfloat16)
        .reshape(rows_here, seq_block, KV_HEADS, group_size, HEAD_DIM)
    )
    key_rot = rotate(
        key_pre.reshape(rows_here, seq_block, KV_HEADS, HEAD_DIM), positions, 1.0
    ).astype(jnp.bfloat16)

    def piece_weights(key_piece):
        key_count = key_piece.shape[1]
        key_pos = jnp.arange(key_count, dtype=jnp.int32)
        raw_scores = (
            jnp.einsum(
                "bqgrd,bkgd->bgrqk", query_rot, key_piece, preferred_element_type=jnp.float32
            )
            * score_scale
        )
        allowed = (key_pos[None, :] <= positions[:, None])[None] & (
            doc_ids[:, None, :] == query_docs[:, :, None]
        )
        bent_score = jnp.tanh(raw_scores / softcap)
        weights = jnp.where(allowed[:, None, None], jnp.exp(softcap * bent_score), 0.0)
        return (weights, bent_score)

    key_piece = lax.all_gather(key_rot, "seq", axis=1, tiled=True)
    value_piece = lax.all_gather(value_low, "seq", axis=1, tiled=True)
    weights, bent_score = piece_weights(key_piece)
    summed = jnp.einsum(
        "bgrqk,bkgd->bqgrd",
        weights.astype(jnp.bfloat16),
        value_piece,
        preferred_element_type=jnp.float32,
    )
    totals, summed = (jnp.sum(weights, axis=-1), summed)
    denominator = jnp.transpose(totals, (0, 3, 1, 2))[..., None]
    mixed_out = summed / denominator
    mixed_low = mixed_out.astype(jnp.bfloat16).reshape(token_count, query_width)
    attn_out = jnp.einsum("th,dh->td", mixed_low, proj_full, preferred_element_type=jnp.float32)
    hidden_one = flat_tokens + rmsnorm(attn_out, gain_second)
    mid_low = rmsnorm(hidden_one, gain_third).astype(jnp.bfloat16)
    mid_row = lax.all_gather(mid_low.reshape(rows_here, seq_block, D), "seq", axis=1, tiled=True)
    gate_pre = jnp.einsum("btd,df->btf", mid_row, gate_cols, preferred_element_type=jnp.float32)
    up_pre = jnp.einsum("btd,df->btf", mid_row, up_cols, preferred_element_type=jnp.float32)
    activated = gelu_product(gate_pre, up_pre).astype(jnp.bfloat16)
    ffn_terms = jnp.einsum("btf,df->btd", activated, down_cols, preferred_element_type=jnp.float32)
    ffn_out = lax.psum_scatter(ffn_terms, "seq", scatter_dimension=1, tiled=True).reshape(
        token_count, D
    )
    result = hidden_one + rmsnorm(ffn_out, gain_fourth)
    layer_out = result.astype(jnp.bfloat16).reshape(rows_here, seq_block, D)
    upstream = cotangent.astype(jnp.float32).reshape(token_count, D)
    grad_ffn, fourth_part = jax.vjp(rmsnorm, ffn_out, gain_fourth)[1](upstream)
    grad_ffn_low = grad_ffn.astype(jnp.bfloat16)
    grad_row = lax.all_gather(
        grad_ffn_low.reshape(rows_here, seq_block, D), "seq", axis=1, tiled=True
    )
    grad_act = jnp.einsum("btd,df->btf", grad_row, down_cols, preferred_element_type=jnp.float32)
    grad_gate_pre, grad_up_pre = jax.vjp(gelu_product, gate_pre, up_pre)[1](grad_act)
    grad_gate_low = grad_gate_pre.astype(jnp.bfloat16)
    grad_up_low = grad_up_pre.astype(jnp.bfloat16)
    mid_terms = jnp.einsum(
        "btf,df->btd", grad_gate_low, gate_cols, preferred_element_type=jnp.float32
    ) + jnp.einsum("btf,df->btd", grad_up_low, up_cols, preferred_element_type=jnp.float32)
    grad_mid = lax.psum_scatter(mid_terms, "seq", scatter_dimension=1, tiled=True).reshape(
        token_count, D
    )
    column_terms = jnp.stack(
        [
            jnp.einsum("btd,btf->df", mid_row, grad_gate_low, preferred_element_type=jnp.float32),
            jnp.einsum("btd,btf->df", mid_row, grad_up_low, preferred_element_type=jnp.float32),
            jnp.einsum("btd,btf->df", grad_row, activated, preferred_element_type=jnp.float32),
        ]
    )
    returned = lax.all_to_all(
        column_terms.reshape(3, D, 1, col_width).astype(jnp.bfloat16),
        ("rows", "seq"),
        split_axis=1,
        concat_axis=2,
        tiled=True,
    ).astype(jnp.float32)
    column_sums = jnp.sum(
        returned.reshape(3, local_rows, row_groups, seq_count, col_width), axis=2
    ).reshape(3, local_rows, FF)
    hidden_part, third_part = jax.vjp(rmsnorm, hidden_one, gain_third)[1](grad_mid)
    grad_hidden = upstream + hidden_part
    grad_attn, second_part = jax.vjp(rmsnorm, attn_out, gain_second)[1](grad_hidden)
    grad_attn_low = grad_attn.astype(jnp.bfloat16)
    query_back, key_back, value_back, proj_back = (
        lax.all_gather(query_local, ("rows", "seq"), axis=0, tiled=True),
        lax.all_gather(key_local, ("rows", "seq"), axis=0, tiled=True),
        lax.all_gather(value_local, ("rows", "seq"), axis=0, tiled=True),
        lax.all_gather(proj_local, ("rows", "seq"), axis=0, tiled=True),
    )
    grad_mixed = jnp.dot(grad_attn_low, proj_back, preferred_element_type=jnp.float32).reshape(
        rows_here, seq_block, KV_HEADS, group_size, HEAD_DIM
    )
    grad_summed = (grad_mixed / denominator).astype(jnp.bfloat16)
    delta_rows = jnp.transpose(
        jnp.sum(grad_mixed * mixed_out, axis=-1) / denominator[..., 0], (0, 2, 3, 1)
    )
    key_piece = lax.all_gather(key_rot, "seq", axis=1, tiled=True)
    value_piece = lax.all_gather(value_low, "seq", axis=1, tiled=True)
    key_count = key_piece.shape[1]
    weights, bent_score = piece_weights(key_piece)
    grad_weights = (
        jnp.einsum(
            "bqgrd,bkgd->bgrqk", grad_summed, value_piece, preferred_element_type=jnp.float32
        )
        - delta_rows[..., None]
    )
    grad_raw = (weights * grad_weights * (1.0 - bent_score * bent_score)).astype(jnp.bfloat16)
    grad_queries = (
        jnp.einsum("bgrqk,bkgd->bqgrd", grad_raw, key_piece, preferred_element_type=jnp.float32)
        * score_scale
    )
    key_term = (
        jnp.einsum("bgrqk,bqgrd->bkgd", grad_raw, query_rot, preferred_element_type=jnp.float32)
        * score_scale
    )
    value_term = jnp.einsum(
        "bgrqk,bqgrd->bkgd",
        weights.astype(jnp.bfloat16),
        grad_summed,
        preferred_element_type=jnp.float32,
    )
    key_sums = key_term
    value_sums = value_term
    grad_query_rot, key_sums, value_sums = (grad_queries, key_sums, value_sums)
    grad_key_rot, grad_value_sum = (
        lax.psum_scatter(key_sums, "seq", scatter_dimension=1, tiled=True),
        lax.psum_scatter(value_sums, "seq", scatter_dimension=1, tiled=True),
    )
    grad_query_pre = (
        rotate(grad_query_rot.reshape(rows_here, seq_block, HEADS, HEAD_DIM), positions, -1.0)
        .astype(jnp.bfloat16)
        .reshape(token_count, query_width)
    )
    grad_key_pre = (
        rotate(grad_key_rot, positions, -1.0).astype(jnp.bfloat16).reshape(token_count, key_width)
    )
    grad_value_low = grad_value_sum.astype(jnp.bfloat16).reshape(token_count, key_width)
    grad_in = (
        jnp.einsum("tf,df->td", grad_query_pre, query_back, preferred_element_type=jnp.float32)
        + jnp.einsum("tf,df->td", grad_key_pre, key_back, preferred_element_type=jnp.float32)
        + jnp.einsum("tf,df->td", grad_value_low, value_back, preferred_element_type=jnp.float32)
    )
    tokens_part, first_part = jax.vjp(rmsnorm, flat_tokens, gain_first)[1](grad_in)
    grad_tokens = (grad_hidden + tokens_part).reshape(rows_here, seq_block, D)

    def outer_sum(left_side, right_side):
        return jnp.einsum("td,tf->df", left_side, right_side, preferred_element_type=jnp.float32)

    gain_terms = jnp.stack([first_part, second_part, third_part, fourth_part], axis=1)
    padding = jnp.zeros((D, 124), jnp.float32)
    weight_terms = jnp.concatenate(
        [
            outer_sum(normed_low, grad_query_pre),
            outer_sum(normed_low, grad_key_pre),
            outer_sum(normed_low, grad_value_low),
            outer_sum(grad_attn_low, mixed_low),
            gain_terms,
            padding,
        ],
        axis=1,
    )
    summed_terms = lax.psum_scatter(weight_terms, ("rows", "seq"), scatter_dimension=0, tiled=True)
    widths = [query_width, key_width, key_width, query_width]
    pieces_out = []
    column = 0
    for span_cols in widths:
        pieces_out.append(summed_terms[:, column : column + span_cols])
        column = column + span_cols
    return (
        layer_out,
        grad_tokens,
        pieces_out[0],
        pieces_out[1],
        pieces_out[2],
        pieces_out[3],
        column_sums[0],
        column_sums[1],
        column_sums[2],
        summed_terms[:, column],
        summed_terms[:, column + 1],
        summed_terms[:, column + 2],
        summed_terms[:, column + 3],
    )


AXES = ("rows", "seq")
LINE = 4


def moves(places, rule):
    found = []
    for index in range(places):
        y, rest = divmod(index, LINE * 4)
        z, x, c = rest // 4, (rest // 2) % 2, rest % 2
        target = rule(y, z, x, c)
        if target is not None:
            y_to, z_to, x_to, c_to = target
            found.append((index, y_to * LINE * 4 + (z_to * 2 + x_to) * 2 + c_to))
    return found


def send(value, rule):
    return lax.ppermute(value, AXES, moves(2 * LINE * 4, rule))


def to_row(value):
    return send(value, lambda y, z, x, c: (1 - y, z, x, c))


def to_x(value):
    return send(value, lambda y, z, x, c: (y, z, 1 - x, c))


def to_core(value):
    return send(value, lambda y, z, x, c: (y, z, x, 1 - c))


def to_pair(value):
    return send(value, lambda y, z, x, c: (y, z ^ 1, x, c))


def across_middle(value):
    return send(value, lambda y, z, x, c: (y, 3 - z, x, c) if z in (1, 2) else None)


def to_ends(value):
    return send(value, lambda y, z, x, c: (y, z ^ 1, x, c) if z in (1, 2) else None)


def from_ends(value):
    return send(value, lambda y, z, x, c: (y, z ^ 1, x, c) if z in (0, 3) else None)


def up_line(value):
    return send(value, lambda y, z, x, c: (y, z + 1, x, c) if z < LINE - 1 else None)


def down_line(value):
    return send(value, lambda y, z, x, c: (y, z - 1, x, c) if z > 0 else None)


def to_chip(value, dz, dx):
    return send(value, lambda y, z, x, c: (y, z ^ dz, x ^ dx, c))


def low(value):
    return value.astype(jnp.bfloat16)


def wide(value):
    return value.astype(jnp.float32)


def pick(array, index, axis=0):
    return lax.dynamic_index_in_dim(array, index, axis, keepdims=False)


def place(array, piece, starts):
    return lax.dynamic_update_slice(array, piece, starts)


class Spot:
    def __init__(self):
        self.y = lax.axis_index("rows")
        index = lax.axis_index("seq")
        self.z = index // 4
        self.x = (index // 2) % 2
        self.c = index % 2
        self.middle = (self.z == 1) | (self.z == 2)
        upper = self.z >= 2
        self.slots = [
            self.z,
            self.z ^ 1,
            jnp.where(upper, 1, 2).astype(jnp.int32),
            jnp.where(upper, 0, 3).astype(jnp.int32),
        ]


def gather_line(spot, own):
    pair = to_pair(own)
    near = across_middle(own)
    far = across_middle(pair)
    near_end = to_ends(near)
    far_end = to_ends(far)
    return [
        own,
        pair,
        jnp.where(spot.middle, near, near_end),
        jnp.where(spot.middle, far, far_end),
    ]


def reduce_line(parts):
    far = parts[3] + wide(from_ends(low(parts[3])))
    near = parts[2] + wide(from_ends(low(parts[2])))
    pair = parts[1] + wide(across_middle(low(far)))
    own = parts[0] + wide(across_middle(low(near)))
    return own + wide(to_pair(low(pair)))


def gather_group(own):
    over_x = to_x(own)
    return jnp.concatenate([own, to_core(own), over_x, to_core(over_x)], axis=0)


def reduce_group(parts):
    both = wide(parts[:, 0]) + wide(to_core(parts[:, 1]))
    return both[0] + wide(to_x(low(both[1])))


def gather_plane(spot, own):
    return [
        jnp.concatenate([block, to_x(block)], axis=0) for block in gather_line(spot, own)
    ]


def reduce_plane(chunks):
    parts = [None] * LINE
    for slot in (3, 2, 1, 0):
        parts[slot] = wide(chunks[slot][0]) + wide(to_x(chunks[slot][1]))
    return reduce_line(parts)


def member(spot, dx, dc):
    return (spot.x ^ dx) * 2 + (spot.c ^ dc)


def narrow_hidden(spot, sums):
    width = sums.shape[1]
    rows = sums.shape[0] // (2 * LINE * 4)
    blocks = sums.reshape(2, LINE * 2, 2, rows, width)
    cores = low(
        wide(pick(blocks, spot.c, 2)) + wide(to_core(pick(blocks, 1 - spot.c, 2)))
    )
    return low(wide(pick(cores, spot.y)) + wide(to_row(pick(cores, 1 - spot.y))))


GROUP = ((0, 0), (0, 1), (1, 0), (1, 1))
PLANE = ((2, 0), (1, 0), (3, 0), (0, 1), (2, 1), (1, 1), (3, 1))


def my_place():
    index = lax.axis_index("seq")
    return lax.axis_index("rows"), index // 4, (index // 2) % 2, index % 2


def along_line(z, step):
    return (z, z + 1 - 2 * (z % 2), (z + 2) % LINE, LINE - 1 - z)[step]


def device_at(y, z, x, c):
    return (y, (z * 2 + x) * 2 + c)


def under(condition, action):
    if condition is None:
        action()
    else:
        pl.when(condition)(action)


class Courier:
    def __init__(self, send_sem, recv_sem):
        self.send_sem = send_sem
        self.recv_sem = recv_sem
        self.names = {}
        self.sent = []

    def copy(self, source, target, device, name):
        slot = self.names.setdefault(name, len(self.names))
        return pltpu.make_async_remote_copy(
            src_ref=source,
            dst_ref=target,
            send_sem=self.send_sem.at[slot],
            recv_sem=self.recv_sem.at[slot],
            device_id=device,
            device_id_type=pl.DeviceIdType.MESH,
        )

    def send(self, source, target, device, name, condition=None):
        copy = self.copy(source, target, device, name)
        under(condition, copy.start)
        self.sent.append((copy, condition))

    def arrive(self, target, device, name, condition=None):
        under(condition, self.copy(target, target, device, name).wait_recv)

    def finish(self):
        for copy, condition in self.sent:
            under(condition, copy.wait_send)


def greet(devices):
    barrier = pltpu.get_barrier_semaphore()
    for device in devices:
        pl.semaphore_signal(
            barrier, inc=1, device_id=device, device_id_type=pl.DeviceIdType.MESH
        )
    pl.semaphore_wait(barrier, len(devices))


def gather_kernel(count, *refs):
    heads_in, tokens_in = refs[:2]
    hidden_in = refs[2 : 2 + count]
    heads, tokens = refs[2 + count : 4 + count]
    hidden = refs[4 + count : 4 + 2 * count]
    send_sem, recv_sem, local_sem = refs[4 + 2 * count :]
    y, z, x, c = my_place()
    me = x * 2 + c
    chip = z * 2 + x
    chips = LINE * 2
    group = {d: device_at(y, z, (x + d[0]) % 2, (c + d[1]) % 2) for d in GROUP[1:]}
    plane = {d: device_at(y, along_line(z, d[0]), (x + d[1]) % 2, c) for d in PLANE}
    row_peer = device_at(1 - y, z, x, c)
    core_peer = group[(0, 1)]
    up = device_at(y, jnp.minimum(z + 1, LINE - 1), x, c)
    down = device_at(y, jnp.maximum(z - 1, 0), x, c)
    can_up = z < LINE - 1
    can_down = z > 0
    greet([row_peer, core_peer, group[(1, 1)]] + list(plane.values()))
    post = Courier(send_sem, recv_sem)

    def member(d):
        return ((x + d[0]) % 2) * 2 + (c + d[1]) % 2

    def chip_of(d):
        return along_line(z, d[0]) * 2 + (x + d[1]) % 2

    def columns(ref, which):
        width = ref.shape[1] // chips
        return ref.at[:, pl.ds(pl.multiple_of(which * width, 128), width)]

    for d, device in group.items():
        post.send(heads_in.at[member(d)], heads.at[y, z, me], device, ("group", d))
    local = [(heads_in.at[me], heads.at[y, z, me]), (tokens_in, tokens.at[0])]
    local += [(columns(w, chip), out.at[y, chip, c]) for w, out in zip(hidden_in, hidden)]
    kept = []
    for slot, (source, target) in enumerate(local):
        kept.append(pltpu.make_async_copy(source, target, local_sem.at[slot]))
        kept[-1].start()
    for d, device in group.items():
        post.send(tokens_in, tokens.at[d[0] * 2 + d[1]], device, ("tokens", d))

    def spread(source, which):
        target = heads.at[y, z, member(which)]
        post.send(source, target, up, ("up", 1, which), can_up)
        post.send(source, target, down, ("down", 1, which), can_down)
        post.send(source, target, row_peer, ("row", 0, 0, which))

    def plane_out(m):
        for d in PLANE:
            post.send(
                columns(hidden_in[m], chip_of(d)),
                hidden[m].at[y, chip, c],
                plane[d],
                ("plane", m, d),
            )
        own = columns(hidden_in[m], chip)
        post.send(own, hidden[m].at[y, chip, c], row_peer, ("far", m, (0, 0)))
        post.send(own, hidden[m].at[y, chip, c], core_peer, ("core", 0, m, (0, 0)))

    def plane_in(m):
        for d in PLANE:
            block = hidden[m].at[y, chip_of(d), c]
            post.arrive(block, core_peer, ("plane", m, d))
            post.send(block, block, row_peer, ("far", m, d))
            post.send(block, block, core_peer, ("core", 0, m, d))

    spread(heads_in.at[me], (0, 0))
    if count:
        plane_out(0)
    for d in GROUP[1:]:
        block = heads.at[y, z, member(d)]
        post.arrive(block, core_peer, ("group", d))
        spread(block, d)
    sides = ((-1, "up", up, can_up), (1, "down", down, can_down))
    for step in range(1, LINE):
        for d in GROUP:
            for sign, name, device, onward in sides:
                here = z >= step if sign < 0 else z <= LINE - 1 - step
                block = heads.at[y, jnp.clip(z + sign * step, 0, LINE - 1), member(d)]
                post.arrive(block, core_peer, (name, step, d), here)
                if step < LINE - 1:
                    post.send(block, block, device, (name, step + 1, d), here & onward)
                post.send(block, block, row_peer, ("row", sign, step, d), here)
        if step == 1 and count:
            plane_in(0)
            if count > 1:
                plane_out(1)
    for m in range(1, count):
        if m + 1 < count:
            plane_out(m + 1)
        plane_in(m)
    for m in range(count):
        for d in ((0, 0),) + PLANE:
            block = hidden[m].at[1 - y, chip_of(d), c]
            post.arrive(block, core_peer, ("far", m, d))
            post.send(block, block, core_peer, ("core", 1, m, d))
    for d in GROUP[1:]:
        post.arrive(tokens.at[d[0] * 2 + d[1]], core_peer, ("tokens", d))
    for d in GROUP:
        post.arrive(heads.at[1 - y, z, member(d)], core_peer, ("row", 0, 0, d))
        for step in range(1, LINE):
            for sign, name, device, onward in sides:
                here = z >= step if sign < 0 else z <= LINE - 1 - step
                block = heads.at[1 - y, jnp.clip(z + sign * step, 0, LINE - 1), member(d)]
                post.arrive(block, core_peer, ("row", sign, step, d), here)
    for m in range(count):
        for half in range(2):
            for d in ((0, 0),) + PLANE:
                block = hidden[m].at[y if half == 0 else 1 - y, chip_of(d), 1 - c]
                post.arrive(block, core_peer, ("core", half, m, d))
    post.finish()
    for copy in kept:
        copy.wait()


def gather_weights(heads_in, tokens_in, hidden_in):
    rows = heads_in.shape[1]
    count = len(hidden_in)
    anywhere = pl.BlockSpec(memory_space=pl.ANY)
    copies = 44 + 4 * len(GROUP) + (7 + 24) * count
    outs = [
        jax.ShapeDtypeStruct((2, LINE, 4, rows, heads_in.shape[2]), jnp.bfloat16),
        jax.ShapeDtypeStruct((4,) + tokens_in.shape, jnp.bfloat16),
    ]
    for matrix in hidden_in:
        width = matrix.shape[1] // (LINE * 2)
        outs.append(jax.ShapeDtypeStruct((2, LINE * 2, 2, rows, width), jnp.bfloat16))
    found = pl.pallas_call(
        functools.partial(gather_kernel, count),
        out_shape=outs,
        in_specs=[anywhere] * (2 + count),
        out_specs=[anywhere] * (2 + count),
        scratch_shapes=[
            pltpu.SemaphoreType.DMA((copies,)),
            pltpu.SemaphoreType.DMA((copies,)),
            pltpu.SemaphoreType.DMA((2 + count,)),
        ],
        compiler_params=pltpu.CompilerParams(collective_id=0, has_side_effects=True),
    )(heads_in, tokens_in, *hidden_in)
    total = 2 * LINE * 4 * rows
    heads = found[0].reshape(total, heads_in.shape[2])
    tokens = found[1].reshape(4 * tokens_in.shape[0], tokens_in.shape[1])
    return heads, tokens, [block.reshape(total, block.shape[-1]) for block in found[2:]]


def scatter_kernel(parts, count, *refs):
    heads_in = refs[:parts]
    hidden_in = refs[parts : parts + count]
    heads = refs[parts + count : 2 * parts + count]
    hidden = refs[2 * parts + count : 2 * (parts + count)]
    scratch = refs[2 * (parts + count) :]
    own, across, above, below = (scratch[n * parts : (n + 1) * parts] for n in range(4))
    send_sem, recv_sem, load_sem, head_send, head_recv, local_sem = scratch[4 * parts :]
    y, z, x, c = my_place()
    me = x * 2 + c
    chip = z * 2 + x
    chips = LINE * 2
    group = {d: device_at(y, z, (x + d[0]) % 2, (c + d[1]) % 2) for d in GROUP[1:]}
    plane = {d: device_at(y, along_line(z, d[0]), (x + d[1]) % 2, c) for d in PLANE}
    row_peer = device_at(1 - y, z, x, c)
    core_peer = group[(0, 1)]
    up = device_at(y, jnp.minimum(z + 1, LINE - 1), x, c)
    down = device_at(y, jnp.maximum(z - 1, 0), x, c)
    greet([row_peer, core_peer, group[(1, 1)]] + list(plane.values()))
    post = Courier(send_sem, recv_sem)

    def member(d):
        return ((x + d[0]) % 2) * 2 + (c + d[1]) % 2

    def chip_of(d):
        return along_line(z, d[0]) * 2 + (x + d[1]) % 2

    order = [(0, 0, None)]
    for step in range(1, LINE):
        order = [(1, step, z <= LINE - 1 - step), (-1, step, z >= step)] + order

    def head_copy(p, stage, source, target, device, place, m):
        return pltpu.make_async_remote_copy(
            src_ref=source,
            dst_ref=target,
            send_sem=head_send.at[p, stage, place, m],
            recv_sem=head_recv.at[p, stage, place, m],
            device_id=device,
            device_id_type=pl.DeviceIdType.MESH,
        )

    def to_row_copy(p, place, m):
        return head_copy(
            p, 0, heads_in[p].at[1 - y, place, m], across[p].at[place, m], row_peer, place, m
        )

    def load_copy(p, place, m):
        return pltpu.make_async_copy(
            heads_in[p].at[y, place, m], own[p].at[place, m], load_sem.at[p, place, m]
        )

    def up_copy(p, place, m):
        return head_copy(p, 1, own[p].at[place, m], below[p].at[place, m], up, place, m)

    def down_copy(p, place, m):
        return head_copy(p, 2, own[p].at[place, m], above[p].at[place, m], down, place, m)

    def each(action):
        lax.fori_loop(0, 4, lambda m, carry: (action(m), carry)[1], 0)

    for sign, step, okay in order:
        place = z + sign * step

        def start(m, place=place):
            for p in range(parts):
                to_row_copy(p, place, m).start()
                load_copy(p, place, m).start()

        under(okay, lambda start=start: each(start))
    kept = []
    for m in range(count):
        for d in PLANE:
            width = hidden[m].shape[1] // chips
            post.send(
                hidden_in[m].at[chip_of(d)],
                hidden[m].at[:, pl.ds(pl.multiple_of(chip * width, 128), width)],
                plane[d],
                ("plane", m, d),
            )
        kept.append(
            pltpu.make_async_copy(
                hidden_in[m].at[chip],
                hidden[m].at[:, pl.ds(pl.multiple_of(chip * width, 128), width)],
                local_sem.at[m],
            )
        )
        kept[-1].start()

    def ready(p, place, m):
        to_row_copy(p, place, m).wait_recv()
        load_copy(p, place, m).wait()
        return wide(own[p][place, m]) + wide(across[p][place, m])

    for sign, step, okay in order[:-1]:
        place = z + sign * step

        def relay(m, place=place, sign=sign):
            for p in range(parts):
                own[p][place, m] = low(ready(p, place, m))
            if sign > 0:
                @pl.when(z > 0)
                def _():
                    for p in range(parts):
                        up_copy(p, place, m).wait_recv()
                        own[p][place, m] = low(wide(own[p][place, m]) + wide(below[p][place, m]))
            else:
                @pl.when(z < LINE - 1)
                def _():
                    for p in range(parts):
                        down_copy(p, place, m).wait_recv()
                        own[p][place, m] = low(wide(own[p][place, m]) + wide(above[p][place, m]))
            for p in range(parts):
                (up_copy if sign > 0 else down_copy)(p, place, m).start()

        under(okay, lambda relay=relay: each(relay))

    def settle(m):
        for p in range(parts):
            own[p][z, m] = low(ready(p, z, m))

        @pl.when(z > 0)
        def _():
            for p in range(parts):
                up_copy(p, z, m).wait_recv()
                own[p][z, m] = low(wide(own[p][z, m]) + wide(below[p][z, m]))

        @pl.when(z < LINE - 1)
        def _():
            for p in range(parts):
                down_copy(p, z, m).wait_recv()
                own[p][z, m] = low(wide(own[p][z, m]) + wide(above[p][z, m]))

    each(settle)
    for p in range(parts):
        kept.append(pltpu.make_async_copy(own[p].at[z, me], heads[p].at[me], local_sem.at[count + p]))
        kept[-1].start()
        for d, device in group.items():
            post.send(own[p].at[z, member(d)], heads[p].at[me], device, ("group", p, d))
    for p in range(parts):
        for d in GROUP[1:]:
            post.arrive(heads[p].at[member(d)], core_peer, ("group", p, d))
    for m in range(count):
        for d in PLANE:
            width = hidden[m].shape[1] // chips
            block = hidden[m].at[:, pl.ds(pl.multiple_of(chip_of(d) * width, 128), width)]
            post.arrive(block, core_peer, ("plane", m, d))
    for sign, step, okay in order:
        place = z + sign * step

        def drain(m, place=place, sign=sign):
            for p in range(parts):
                to_row_copy(p, place, m).wait_send()
                if sign > 0:
                    up_copy(p, place, m).wait_send()
                if sign < 0:
                    down_copy(p, place, m).wait_send()

        under(okay, lambda drain=drain: each(drain))
    post.finish()
    for copy in kept:
        copy.wait()


def scatter_weights(head_sums, hidden_sums):
    parts, count = len(head_sums), len(hidden_sums)
    rows = head_sums[0].shape[0] // (2 * LINE * 4)
    anywhere = pl.BlockSpec(memory_space=pl.ANY)
    copies = 7 * count + 3 * parts
    outs = [jax.ShapeDtypeStruct((4, rows, h.shape[1]), jnp.bfloat16) for h in head_sums]
    outs += [
        jax.ShapeDtypeStruct((rows, h.shape[0] * h.shape[2]), jnp.bfloat16) for h in hidden_sums
    ]
    found = pl.pallas_call(
        functools.partial(scatter_kernel, parts, count),
        out_shape=outs,
        in_specs=[anywhere] * (parts + count),
        out_specs=[anywhere] * (parts + count),
        scratch_shapes=[
            pltpu.VMEM((LINE, 4, rows, h.shape[1]), jnp.bfloat16) for _ in range(4) for h in head_sums
        ]
        + [
            pltpu.SemaphoreType.DMA((copies,)),
            pltpu.SemaphoreType.DMA((copies,)),
            pltpu.SemaphoreType.DMA((parts, LINE, 4)),
            pltpu.SemaphoreType.DMA((parts, 3, LINE, 4)),
            pltpu.SemaphoreType.DMA((parts, 3, LINE, 4)),
            pltpu.SemaphoreType.DMA((count + parts,)),
        ],
        compiler_params=pltpu.CompilerParams(
            collective_id=1, has_side_effects=True, vmem_limit_bytes=40 << 20
        ),
    )(
        *[h.reshape(2, LINE, 4, rows, h.shape[1]) for h in head_sums],
        *hidden_sums,
    )
    return found[:parts], found[parts:]


def scatter_gains(spot, gains):
    count = gains.shape[0]
    left = gains.reshape(count, 2, 2, 2, 2, 2, -1)
    for bit, rule in (
        (spot.y, to_row),
        (spot.z // 2, lambda v: to_chip(v, 2, 0)),
        (spot.z % 2, lambda v: to_chip(v, 1, 0)),
        (spot.x, to_x),
        (spot.c, to_core),
    ):
        left = pick(left, bit, 1) + rule(pick(left, 1 - bit, 1))
    return left


def split_columns(matrix, count):
    rows, cols = matrix.shape
    return matrix.reshape(rows, count, cols // count).transpose(1, 0, 2)


def join_columns(blocks):
    count, rows, cols = blocks.shape
    return wide(blocks).transpose(1, 0, 2).reshape(rows, count * cols)


def turn(values, cosine, sine):
    half_dim = HEAD_DIM // 2
    front_half = values[..., :half_dim]
    back_half = values[..., half_dim:]
    return jnp.concatenate(
        [front_half * cosine - back_half * sine, back_half * cosine + front_half * sine], axis=-1
    )


def dot(left_side, right_side):
    return jnp.dot(left_side, right_side, preferred_element_type=jnp.float32)


def dot_rows(left_side, right_side):
    return jnp.einsum("tf,df->td", left_side, right_side, preferred_element_type=jnp.float32)


def outer_sum(left_side, right_side):
    return jnp.einsum("td,tf->df", left_side, right_side, preferred_element_type=jnp.float32)


def per_device_line(
    tokens,
    cotangent,
    doc_ids,
    bit_levels,
    w_query,
    w_key,
    w_value,
    w_proj,
    w_gate,
    w_up,
    w_down,
    gain_first,
    gain_second,
    gain_third,
    gain_fourth,
):
    spot = Spot()
    count = tokens.shape[1]
    group_size = HEADS // KV_HEADS
    query_width = HEADS * HEAD_DIM
    score_scale = HEAD_DIM ** (-0.5)
    span = 4 * count

    heads_in = low(
        jnp.concatenate(
            [
                split_columns(dequant(w_query, bit_levels[0], D, qk_boost), KV_HEADS),
                split_columns(dequant(w_key, bit_levels[1], D, qk_boost), KV_HEADS),
                split_columns(dequant(w_value, bit_levels[2], D, 1.0), KV_HEADS),
                split_columns(dequant(w_proj, bit_levels[3], query_width, 1.0), KV_HEADS),
            ],
            axis=2,
        )
    )
    flat_tokens = wide(tokens).reshape(count, D)
    normed_low = low(rmsnorm(flat_tokens, gain_first))
    all_heads, normed_all, (gate_w, up_w, down_w) = gather_weights(
        heads_in,
        normed_low,
        [
            low(dequant(w_gate, bit_levels[4], D, 1.0)),
            low(dequant(w_up, bit_levels[5], D, 1.0)),
            low(dequant(w_down, bit_levels[6], FF, 1.0)),
        ],
    )
    head_width = (group_size + 2) * HEAD_DIM
    heads_w = all_heads[:, :head_width]
    proj_w = all_heads[:, head_width:]

    inner = jnp.arange(count, dtype=jnp.int32)
    offsets = jnp.concatenate(
        [member(spot, dx, dc) * count + inner for dx in range(2) for dc in range(2)]
    )
    positions = spot.z * span + offsets
    half_dim = HEAD_DIM // 2
    frequency = 10000.0 ** (-(2.0 / HEAD_DIM) * jnp.arange(half_dim, dtype=jnp.float32))
    angles = positions.astype(jnp.float32)[:, None] * frequency[None, :]
    cosine = jnp.cos(angles)
    sine = jnp.sin(angles)
    docs = doc_ids.reshape(LINE, 2, 2, count)
    docs = jnp.where(spot.x == 1, docs[:, ::-1], docs)
    docs = jnp.where(spot.c == 1, docs[:, :, ::-1], docs).reshape(LINE, span)
    query_docs = pick(docs, spot.z)

    pre = dot(normed_all, heads_w)
    wide_q = group_size * HEAD_DIM
    query_rot = low(
        turn(
            pre[:, :wide_q].reshape(span, group_size, HEAD_DIM),
            cosine[:, None],
            sine[:, None],
        )
    )
    key_rot = low(turn(pre[:, wide_q : wide_q + HEAD_DIM], cosine, sine))
    value_low = low(pre[:, wide_q + HEAD_DIM :])
    key_value = [jnp.concatenate([key_rot, value_low], axis=1)]
    for _ in range(1, LINE):
        key_value.append(up_line(key_value[-1]))

    totals = 0.0
    summed = 0.0
    saved = []
    for back, block in enumerate(key_value):
        key_piece, value_piece = block[:, :HEAD_DIM], block[:, HEAD_DIM:]
        key_docs = pick(docs, jnp.maximum(spot.z - back, 0))
        key_pos = positions - back * span
        allowed = (
            (key_pos[None, :] <= positions[:, None])
            & (key_pos[None, :] >= 0)
            & (key_docs[None, :] == query_docs[:, None])
        )
        raw_scores = (
            jnp.einsum("qrd,kd->rqk", query_rot, key_piece, preferred_element_type=jnp.float32)
            * score_scale
        )
        bent = jnp.tanh(raw_scores / softcap)
        weights = jnp.where(allowed[None], jnp.exp(softcap * bent), 0.0)
        totals = totals + jnp.sum(weights, axis=-1)
        summed = summed + jnp.einsum(
            "rqk,kd->qrd", low(weights), value_piece, preferred_element_type=jnp.float32
        )
        saved.append((key_piece, value_piece, weights, bent))
    denominator = jnp.transpose(totals)[..., None]
    mixed_out = summed / denominator
    mixed_low = low(mixed_out).reshape(span, wide_q)
    attn_out = reduce_group(low(dot_rows(mixed_low, proj_w)).reshape(2, 2, count, D))
    hidden_one = flat_tokens + rmsnorm(attn_out, gain_second)
    mid_low = low(rmsnorm(hidden_one, gain_third))

    mid_chunks = gather_plane(spot, mid_low)
    gates, acts, ffn_chunks = [], [], []
    for chunk in mid_chunks:
        gate_pre = dot(chunk, gate_w)
        up_pre = dot(chunk, up_w)
        activated = low(gelu_product(gate_pre, up_pre))
        gates.append((gate_pre, up_pre))
        acts.append(activated)
        ffn_chunks.append(low(dot_rows(activated, down_w)).reshape(2, count, D))
    ffn_out = reduce_plane(ffn_chunks)
    result = hidden_one + rmsnorm(ffn_out, gain_fourth)
    layer_out = low(result).reshape(1, count, D)

    upstream = wide(cotangent).reshape(count, D)
    grad_ffn, fourth_part = jax.vjp(rmsnorm, ffn_out, gain_fourth)[1](upstream)
    grad_chunks = gather_plane(spot, low(grad_ffn))
    gate_grads, up_grads, back_chunks = [], [], []
    for chunk, (gate_pre, up_pre) in zip(grad_chunks, gates):
        grad_act = dot(chunk, down_w)
        grad_gate_pre, grad_up_pre = jax.vjp(gelu_product, gate_pre, up_pre)[1](grad_act)
        gate_grads.append(low(grad_gate_pre))
        up_grads.append(low(grad_up_pre))
        back_chunks.append(
            low(dot_rows(gate_grads[-1], gate_w) + dot_rows(up_grads[-1], up_w)).reshape(
                2, count, D
            )
        )
    grad_mid = reduce_plane(back_chunks)
    mid_all = jnp.concatenate(mid_chunks, axis=0)
    gate_sums = narrow_hidden(spot, low(outer_sum(mid_all, jnp.concatenate(gate_grads, axis=0))))
    up_sums = narrow_hidden(spot, low(outer_sum(mid_all, jnp.concatenate(up_grads, axis=0))))
    down_sums = narrow_hidden(
        spot,
        low(outer_sum(jnp.concatenate(grad_chunks, axis=0), jnp.concatenate(acts, axis=0))),
    )

    hidden_part, third_part = jax.vjp(rmsnorm, hidden_one, gain_third)[1](grad_mid)
    grad_hidden = upstream + hidden_part
    grad_attn, second_part = jax.vjp(rmsnorm, attn_out, gain_second)[1](grad_hidden)
    grad_attn_all = gather_group(low(grad_attn))
    proj_sums = low(outer_sum(grad_attn_all, mixed_low))
    late_gains = scatter_gains(spot, jnp.stack([second_part, third_part, fourth_part]))

    grad_mixed = dot(grad_attn_all, proj_w).reshape(span, group_size, HEAD_DIM)
    grad_summed = low(grad_mixed / denominator)
    delta = jnp.transpose(jnp.sum(grad_mixed * mixed_out, axis=-1)) / totals
    grad_query_rot = 0.0
    passed = None
    for back in range(LINE - 1, -1, -1):
        key_piece, value_piece, weights, bent = saved[back]
        grad_weights = (
            jnp.einsum(
                "qrd,kd->rqk", grad_summed, value_piece, preferred_element_type=jnp.float32
            )
            - delta[..., None]
        )
        grad_raw = low(weights * grad_weights * (1.0 - bent * bent))
        grad_query_rot = grad_query_rot + jnp.einsum(
            "rqk,kd->qrd", grad_raw, key_piece, preferred_element_type=jnp.float32
        )
        key_term = (
            jnp.einsum("rqk,qrd->kd", grad_raw, query_rot, preferred_element_type=jnp.float32)
            * score_scale
        )
        value_term = jnp.einsum(
            "rqk,qrd->kd", low(weights), grad_summed, preferred_element_type=jnp.float32
        )
        sums = jnp.concatenate([key_term, value_term], axis=1)
        if passed is not None:
            sums = sums + wide(down_line(passed))
        passed = low(sums)
    grad_query_pre = low(
        turn(grad_query_rot * score_scale, cosine[:, None], -sine[:, None])
    ).reshape(span, wide_q)
    grad_key_pre = low(turn(sums[:, :HEAD_DIM], cosine, -sine))
    grad_pre = jnp.concatenate([grad_query_pre, grad_key_pre, low(sums[:, HEAD_DIM:])], axis=1)
    (head_rows, proj_rows), (grad_gate, grad_up, grad_down) = scatter_weights(
        [low(outer_sum(normed_all, grad_pre)), proj_sums], [gate_sums, up_sums, down_sums]
    )
    grad_in = reduce_group(low(dot_rows(grad_pre, heads_w)).reshape(2, 2, count, D))
    tokens_part, first_part = jax.vjp(rmsnorm, flat_tokens, gain_first)[1](grad_in)
    grad_tokens = (grad_hidden + tokens_part).reshape(1, count, D)

    first_gain = scatter_gains(spot, first_part[None])
    return (
        layer_out,
        grad_tokens,
        join_columns(head_rows[:, :, :wide_q]),
        join_columns(head_rows[:, :, wide_q : wide_q + HEAD_DIM]),
        join_columns(head_rows[:, :, wide_q + HEAD_DIM :]),
        join_columns(proj_rows),
        wide(grad_gate),
        wide(grad_up),
        wide(grad_down),
        first_gain[0],
        late_gains[0],
        late_gains[1],
        late_gains[2],
    )


def solution(mesh):
    placed = (
        P("rows", "seq", None),
        P("rows", "seq", None),
        P("rows", None),
        P(),
        P(("rows", "seq"), None),
        P(("rows", "seq"), None),
        P(("rows", "seq"), None),
        P(("rows", "seq"), None),
        P(("rows", "seq"), None),
        P(("rows", "seq"), None),
        P(("rows", "seq"), None),
        P(),
        P(),
        P(),
        P(),
    )
    sizes = dict(mesh.shape)
    fits = sizes["rows"] == 2 and sizes["seq"] == LINE * 4
    return jax.shard_map(
        per_device_line if fits else per_device_plain,
        mesh=mesh,
        in_specs=placed,
        out_specs=(
            P("rows", "seq", None),
            P("rows", "seq", None),
            P(("rows", "seq"), None),
            P(("rows", "seq"), None),
            P(("rows", "seq"), None),
            P(("rows", "seq"), None),
            P(("rows", "seq"), None),
            P(("rows", "seq"), None),
            P(("rows", "seq"), None),
            P(("rows", "seq")),
            P(("rows", "seq")),
            P(("rows", "seq")),
            P(("rows", "seq")),
        ),
        check_vma=False,
    )
```

```python
import functools
import math

import jax
import jax.numpy as jnp
from jax import lax
from jax.experimental import pallas as pl
from jax.experimental.pallas import tpu as pltpu
from jax.sharding import PartitionSpec as P

D = 2304
FF = 9216
HEADS = 8
KV_HEADS = 4
HEAD_DIM = 256


softcap = 50.0
epsilon = 1e-06
qk_boost = 1.65


def dequant(levels_int, level_idx, fan_in, boost):
    bits = jnp.where(level_idx == 0, 0, jnp.where(level_idx == 1, 4, 6)).astype(jnp.int32)
    middle = jnp.where(level_idx == 0, 0, jnp.where(level_idx == 1, 8, 32)).astype(jnp.int32)
    sliced = ((levels_int >> bits) << bits) + middle
    return sliced.astype(jnp.float32) * (boost / (74.0 * math.sqrt(fan_in)))


def rmsnorm(values, gain_vec):
    return (
        values
        * lax.rsqrt(jnp.mean(values * values, axis=-1, keepdims=True) + epsilon)
        * (1.0 + gain_vec)
    )


def rotate(values, positions, direction):
    half_dim = HEAD_DIM // 2
    frequency = 10000.0 ** (-(2.0 / HEAD_DIM) * jnp.arange(half_dim, dtype=jnp.float32))
    angles = positions.astype(jnp.float32)[:, None] * frequency[None, :]
    cosine = jnp.cos(angles)[:, None, :]
    sine = jnp.sin(angles)[:, None, :] * direction
    front_half = values[..., :half_dim]
    back_half = values[..., half_dim:]
    return jnp.concatenate(
        [front_half * cosine - back_half * sine, back_half * cosine + front_half * sine], axis=-1
    )


def gelu_product(gate_vals, up_vals):
    return jax.nn.gelu(gate_vals, approximate=True) * up_vals


def per_device_plain(
    tokens,
    cotangent,
    doc_ids,
    bit_levels,
    w_query,
    w_key,
    w_value,
    w_proj,
    w_gate,
    w_up,
    w_down,
    gain_first,
    gain_second,
    gain_third,
    gain_fourth,
):
    rows_here = tokens.shape[0]
    seq_block = tokens.shape[1]
    token_count = rows_here * seq_block
    local_rows = w_query.shape[0]
    group_size = HEADS // KV_HEADS
    query_width = HEADS * HEAD_DIM
    key_width = KV_HEADS * HEAD_DIM
    score_scale = HEAD_DIM ** (-0.5)
    offset = lax.axis_index("seq") * seq_block
    positions = offset + jnp.arange(seq_block, dtype=jnp.int32)
    query_docs = lax.dynamic_slice_in_dim(doc_ids, offset, seq_block, 1)
    query_local = dequant(w_query, bit_levels[0], D, qk_boost).astype(jnp.bfloat16)
    key_local = dequant(w_key, bit_levels[1], D, qk_boost).astype(jnp.bfloat16)
    value_local = dequant(w_value, bit_levels[2], D, 1.0).astype(jnp.bfloat16)
    proj_local = dequant(w_proj, bit_levels[3], query_width, 1.0).astype(jnp.bfloat16)
    gate_local = dequant(w_gate, bit_levels[4], D, 1.0).astype(jnp.bfloat16)
    up_local = dequant(w_up, bit_levels[5], D, 1.0).astype(jnp.bfloat16)
    down_local = dequant(w_down, bit_levels[6], FF, 1.0).astype(jnp.bfloat16)
    query_full, key_full, value_full, proj_full = (
        lax.all_gather(query_local, ("rows", "seq"), axis=0, tiled=True),
        lax.all_gather(key_local, ("rows", "seq"), axis=0, tiled=True),
        lax.all_gather(value_local, ("rows", "seq"), axis=0, tiled=True),
        lax.all_gather(proj_local, ("rows", "seq"), axis=0, tiled=True),
    )
    row_groups = lax.axis_size("rows")
    seq_count = lax.axis_size("seq")
    col_width = FF // seq_count
    stacked = jnp.stack([gate_local, up_local, down_local]).reshape(
        3, local_rows, seq_count, col_width
    )
    spread = jnp.concatenate([stacked] * row_groups, axis=2)
    columns_all = lax.all_to_all(
        spread, ("rows", "seq"), split_axis=2, concat_axis=1, tiled=True
    ).reshape(3, D, col_width)
    gate_cols = columns_all[0]
    up_cols = columns_all[1]
    down_cols = columns_all[2]
    flat_tokens = tokens.astype(jnp.float32).reshape(token_count, D)
    normed_low = rmsnorm(flat_tokens, gain_first).astype(jnp.bfloat16)
    query_pre = jnp.dot(normed_low, query_full, preferred_element_type=jnp.float32)
    key_pre = jnp.dot(normed_low, key_full, preferred_element_type=jnp.float32)
    value_low = (
        jnp.dot(normed_low, value_full, preferred_element_type=jnp.float32)
        .astype(jnp.bfloat16)
        .reshape(rows_here, seq_block, KV_HEADS, HEAD_DIM)
    )
    query_rot = (
        rotate(query_pre.reshape(rows_here, seq_block, HEADS, HEAD_DIM), positions, 1.0)
        .astype(jnp.bfloat16)
        .reshape(rows_here, seq_block, KV_HEADS, group_size, HEAD_DIM)
    )
    key_rot = rotate(
        key_pre.reshape(rows_here, seq_block, KV_HEADS, HEAD_DIM), positions, 1.0
    ).astype(jnp.bfloat16)

    def piece_weights(key_piece):
        key_count = key_piece.shape[1]
        key_pos = jnp.arange(key_count, dtype=jnp.int32)
        raw_scores = (
            jnp.einsum(
                "bqgrd,bkgd->bgrqk", query_rot, key_piece, preferred_element_type=jnp.float32
            )
            * score_scale
        )
        allowed = (key_pos[None, :] <= positions[:, None])[None] & (
            doc_ids[:, None, :] == query_docs[:, :, None]
        )
        bent_score = jnp.tanh(raw_scores / softcap)
        weights = jnp.where(allowed[:, None, None], jnp.exp(softcap * bent_score), 0.0)
        return (weights, bent_score)

    key_piece = lax.all_gather(key_rot, "seq", axis=1, tiled=True)
    value_piece = lax.all_gather(value_low, "seq", axis=1, tiled=True)
    weights, bent_score = piece_weights(key_piece)
    summed = jnp.einsum(
        "bgrqk,bkgd->bqgrd",
        weights.astype(jnp.bfloat16),
        value_piece,
        preferred_element_type=jnp.float32,
    )
    totals, summed = (jnp.sum(weights, axis=-1), summed)
    denominator = jnp.transpose(totals, (0, 3, 1, 2))[..., None]
    mixed_out = summed / denominator
    mixed_low = mixed_out.astype(jnp.bfloat16).reshape(token_count, query_width)
    attn_out = jnp.einsum("th,dh->td", mixed_low, proj_full, preferred_element_type=jnp.float32)
    hidden_one = flat_tokens + rmsnorm(attn_out, gain_second)
    mid_low = rmsnorm(hidden_one, gain_third).astype(jnp.bfloat16)
    mid_row = lax.all_gather(mid_low.reshape(rows_here, seq_block, D), "seq", axis=1, tiled=True)
    gate_pre = jnp.einsum("btd,df->btf", mid_row, gate_cols, preferred_element_type=jnp.float32)
    up_pre = jnp.einsum("btd,df->btf", mid_row, up_cols, preferred_element_type=jnp.float32)
    activated = gelu_product(gate_pre, up_pre).astype(jnp.bfloat16)
    ffn_terms = jnp.einsum("btf,df->btd", activated, down_cols, preferred_element_type=jnp.float32)
    ffn_out = lax.psum_scatter(ffn_terms, "seq", scatter_dimension=1, tiled=True).reshape(
        token_count, D
    )
    result = hidden_one + rmsnorm(ffn_out, gain_fourth)
    layer_out = result.astype(jnp.bfloat16).reshape(rows_here, seq_block, D)
    upstream = cotangent.astype(jnp.float32).reshape(token_count, D)
    grad_ffn, fourth_part = jax.vjp(rmsnorm, ffn_out, gain_fourth)[1](upstream)
    grad_ffn_low = grad_ffn.astype(jnp.bfloat16)
    grad_row = lax.all_gather(
        grad_ffn_low.reshape(rows_here, seq_block, D), "seq", axis=1, tiled=True
    )
    grad_act = jnp.einsum("btd,df->btf", grad_row, down_cols, preferred_element_type=jnp.float32)
    grad_gate_pre, grad_up_pre = jax.vjp(gelu_product, gate_pre, up_pre)[1](grad_act)
    grad_gate_low = grad_gate_pre.astype(jnp.bfloat16)
    grad_up_low = grad_up_pre.astype(jnp.bfloat16)
    mid_terms = jnp.einsum(
        "btf,df->btd", grad_gate_low, gate_cols, preferred_element_type=jnp.float32
    ) + jnp.einsum("btf,df->btd", grad_up_low, up_cols, preferred_element_type=jnp.float32)
    grad_mid = lax.psum_scatter(mid_terms, "seq", scatter_dimension=1, tiled=True).reshape(
        token_count, D
    )
    column_terms = jnp.stack(
        [
            jnp.einsum("btd,btf->df", mid_row, grad_gate_low, preferred_element_type=jnp.float32),
            jnp.einsum("btd,btf->df", mid_row, grad_up_low, preferred_element_type=jnp.float32),
            jnp.einsum("btd,btf->df", grad_row, activated, preferred_element_type=jnp.float32),
        ]
    )
    returned = lax.all_to_all(
        column_terms.reshape(3, D, 1, col_width).astype(jnp.bfloat16),
        ("rows", "seq"),
        split_axis=1,
        concat_axis=2,
        tiled=True,
    ).astype(jnp.float32)
    column_sums = jnp.sum(
        returned.reshape(3, local_rows, row_groups, seq_count, col_width), axis=2
    ).reshape(3, local_rows, FF)
    hidden_part, third_part = jax.vjp(rmsnorm, hidden_one, gain_third)[1](grad_mid)
    grad_hidden = upstream + hidden_part
    grad_attn, second_part = jax.vjp(rmsnorm, attn_out, gain_second)[1](grad_hidden)
    grad_attn_low = grad_attn.astype(jnp.bfloat16)
    query_back, key_back, value_back, proj_back = (
        lax.all_gather(query_local, ("rows", "seq"), axis=0, tiled=True),
        lax.all_gather(key_local, ("rows", "seq"), axis=0, tiled=True),
        lax.all_gather(value_local, ("rows", "seq"), axis=0, tiled=True),
        lax.all_gather(proj_local, ("rows", "seq"), axis=0, tiled=True),
    )
    grad_mixed = jnp.dot(grad_attn_low, proj_back, preferred_element_type=jnp.float32).reshape(
        rows_here, seq_block, KV_HEADS, group_size, HEAD_DIM
    )
    grad_summed = (grad_mixed / denominator).astype(jnp.bfloat16)
    delta_rows = jnp.transpose(
        jnp.sum(grad_mixed * mixed_out, axis=-1) / denominator[..., 0], (0, 2, 3, 1)
    )
    key_piece = lax.all_gather(key_rot, "seq", axis=1, tiled=True)
    value_piece = lax.all_gather(value_low, "seq", axis=1, tiled=True)
    key_count = key_piece.shape[1]
    weights, bent_score = piece_weights(key_piece)
    grad_weights = (
        jnp.einsum(
            "bqgrd,bkgd->bgrqk", grad_summed, value_piece, preferred_element_type=jnp.float32
        )
        - delta_rows[..., None]
    )
    grad_raw = (weights * grad_weights * (1.0 - bent_score * bent_score)).astype(jnp.bfloat16)
    grad_queries = (
        jnp.einsum("bgrqk,bkgd->bqgrd", grad_raw, key_piece, preferred_element_type=jnp.float32)
        * score_scale
    )
    key_term = (
        jnp.einsum("bgrqk,bqgrd->bkgd", grad_raw, query_rot, preferred_element_type=jnp.float32)
        * score_scale
    )
    value_term = jnp.einsum(
        "bgrqk,bqgrd->bkgd",
        weights.astype(jnp.bfloat16),
        grad_summed,
        preferred_element_type=jnp.float32,
    )
    key_sums = key_term
    value_sums = value_term
    grad_query_rot, key_sums, value_sums = (grad_queries, key_sums, value_sums)
    grad_key_rot, grad_value_sum = (
        lax.psum_scatter(key_sums, "seq", scatter_dimension=1, tiled=True),
        lax.psum_scatter(value_sums, "seq", scatter_dimension=1, tiled=True),
    )
    grad_query_pre = (
        rotate(grad_query_rot.reshape(rows_here, seq_block, HEADS, HEAD_DIM), positions, -1.0)
        .astype(jnp.bfloat16)
        .reshape(token_count, query_width)
    )
    grad_key_pre = (
        rotate(grad_key_rot, positions, -1.0).astype(jnp.bfloat16).reshape(token_count, key_width)
    )
    grad_value_low = grad_value_sum.astype(jnp.bfloat16).reshape(token_count, key_width)
    grad_in = (
        jnp.einsum("tf,df->td", grad_query_pre, query_back, preferred_element_type=jnp.float32)
        + jnp.einsum("tf,df->td", grad_key_pre, key_back, preferred_element_type=jnp.float32)
        + jnp.einsum("tf,df->td", grad_value_low, value_back, preferred_element_type=jnp.float32)
    )
    tokens_part, first_part = jax.vjp(rmsnorm, flat_tokens, gain_first)[1](grad_in)
    grad_tokens = (grad_hidden + tokens_part).reshape(rows_here, seq_block, D)

    def outer_sum(left_side, right_side):
        return jnp.einsum("td,tf->df", left_side, right_side, preferred_element_type=jnp.float32)

    gain_terms = jnp.stack([first_part, second_part, third_part, fourth_part], axis=1)
    padding = jnp.zeros((D, 124), jnp.float32)
    weight_terms = jnp.concatenate(
        [
            outer_sum(normed_low, grad_query_pre),
            outer_sum(normed_low, grad_key_pre),
            outer_sum(normed_low, grad_value_low),
            outer_sum(grad_attn_low, mixed_low),
            gain_terms,
            padding,
        ],
        axis=1,
    )
    summed_terms = lax.psum_scatter(weight_terms, ("rows", "seq"), scatter_dimension=0, tiled=True)
    widths = [query_width, key_width, key_width, query_width]
    pieces_out = []
    column = 0
    for span_cols in widths:
        pieces_out.append(summed_terms[:, column : column + span_cols])
        column = column + span_cols
    return (
        layer_out,
        grad_tokens,
        pieces_out[0],
        pieces_out[1],
        pieces_out[2],
        pieces_out[3],
        column_sums[0],
        column_sums[1],
        column_sums[2],
        summed_terms[:, column],
        summed_terms[:, column + 1],
        summed_terms[:, column + 2],
        summed_terms[:, column + 3],
    )


AXES = ("rows", "seq")
LINE = 4


def moves(places, rule):
    found = []
    for index in range(places):
        y, rest = divmod(index, LINE * 4)
        z, x, c = rest // 4, (rest // 2) % 2, rest % 2
        target = rule(y, z, x, c)
        if target is not None:
            y_to, z_to, x_to, c_to = target
            found.append((index, y_to * LINE * 4 + (z_to * 2 + x_to) * 2 + c_to))
    return found


def send(value, rule):
    return lax.ppermute(value, AXES, moves(2 * LINE * 4, rule))


def to_row(value):
    return send(value, lambda y, z, x, c: (1 - y, z, x, c))


def to_x(value):
    return send(value, lambda y, z, x, c: (y, z, 1 - x, c))


def to_core(value):
    return send(value, lambda y, z, x, c: (y, z, x, 1 - c))


def to_pair(value):
    return send(value, lambda y, z, x, c: (y, z ^ 1, x, c))


def across_middle(value):
    return send(value, lambda y, z, x, c: (y, 3 - z, x, c) if z in (1, 2) else None)


def to_ends(value):
    return send(value, lambda y, z, x, c: (y, z ^ 1, x, c) if z in (1, 2) else None)


def from_ends(value):
    return send(value, lambda y, z, x, c: (y, z ^ 1, x, c) if z in (0, 3) else None)


def up_line(value):
    return send(value, lambda y, z, x, c: (y, z + 1, x, c) if z < LINE - 1 else None)


def down_line(value):
    return send(value, lambda y, z, x, c: (y, z - 1, x, c) if z > 0 else None)


def to_chip(value, dz, dx):
    return send(value, lambda y, z, x, c: (y, z ^ dz, x ^ dx, c))


def low(value):
    return value.astype(jnp.bfloat16)


def wide(value):
    return value.astype(jnp.float32)


def pick(array, index, axis=0):
    return lax.dynamic_index_in_dim(array, index, axis, keepdims=False)


def place(array, piece, starts):
    return lax.dynamic_update_slice(array, piece, starts)


class Spot:
    def __init__(self):
        self.y = lax.axis_index("rows")
        index = lax.axis_index("seq")
        self.z = index // 4
        self.x = (index // 2) % 2
        self.c = index % 2
        self.middle = (self.z == 1) | (self.z == 2)
        upper = self.z >= 2
        self.slots = [
            self.z,
            self.z ^ 1,
            jnp.where(upper, 1, 2).astype(jnp.int32),
            jnp.where(upper, 0, 3).astype(jnp.int32),
        ]


def gather_line(spot, own):
    pair = to_pair(own)
    near = across_middle(own)
    far = across_middle(pair)
    near_end = to_ends(near)
    far_end = to_ends(far)
    return [
        own,
        pair,
        jnp.where(spot.middle, near, near_end),
        jnp.where(spot.middle, far, far_end),
    ]


def reduce_line(parts):
    far = parts[3] + wide(from_ends(low(parts[3])))
    near = parts[2] + wide(from_ends(low(parts[2])))
    pair = parts[1] + wide(across_middle(low(far)))
    own = parts[0] + wide(across_middle(low(near)))
    return own + wide(to_pair(low(pair)))


def gather_group(own):
    over_x = to_x(own)
    return jnp.concatenate([own, to_core(own), over_x, to_core(over_x)], axis=0)


def reduce_group(parts):
    both = wide(parts[:, 0]) + wide(to_core(parts[:, 1]))
    return both[0] + wide(to_x(low(both[1])))


def gather_plane(spot, own):
    return [
        jnp.concatenate([block, to_x(block)], axis=0) for block in gather_line(spot, own)
    ]


def reduce_plane(chunks):
    parts = [None] * LINE
    for slot in (3, 2, 1, 0):
        if slot == 1:
            parts[3], chunks[1], chunks[0] = lax.optimization_barrier(
                (parts[3], chunks[1], chunks[0])
            )
        parts[slot] = wide(chunks[slot][0]) + wide(to_x(chunks[slot][1]))
    return reduce_line(parts)


def member(spot, dx, dc):
    return (spot.x ^ dx) * 2 + (spot.c ^ dc)


def narrow_hidden(spot, sums):
    width = sums.shape[1]
    rows = sums.shape[0] // (2 * LINE * 4)
    blocks = sums.reshape(2, LINE * 2, 2, rows, width)
    cores = low(
        wide(pick(blocks, spot.c, 2)) + wide(to_core(pick(blocks, 1 - spot.c, 2)))
    )
    return low(wide(pick(cores, spot.y)) + wide(to_row(pick(cores, 1 - spot.y))))


GROUP = ((0, 0), (0, 1), (1, 0), (1, 1))
PLANE = ((2, 0), (1, 0), (3, 0), (0, 1), (2, 1), (1, 1), (3, 1))


def my_place():
    index = lax.axis_index("seq")
    return lax.axis_index("rows"), index // 4, (index // 2) % 2, index % 2


def along_line(z, step):
    return (z, z + 1 - 2 * (z % 2), (z + 2) % LINE, LINE - 1 - z)[step]


def device_at(y, z, x, c):
    return (y, (z * 2 + x) * 2 + c)


def under(condition, action):
    if condition is None:
        action()
    else:
        pl.when(condition)(action)


class Courier:
    def __init__(self, send_sem, recv_sem):
        self.send_sem = send_sem
        self.recv_sem = recv_sem
        self.names = {}
        self.sent = []

    def copy(self, source, target, device, name):
        slot = self.names.setdefault(name, len(self.names))
        return pltpu.make_async_remote_copy(
            src_ref=source,
            dst_ref=target,
            send_sem=self.send_sem.at[slot],
            recv_sem=self.recv_sem.at[slot],
            device_id=device,
            device_id_type=pl.DeviceIdType.MESH,
        )

    def send(self, source, target, device, name, condition=None):
        copy = self.copy(source, target, device, name)
        under(condition, copy.start)
        self.sent.append((copy, condition))

    def arrive(self, target, device, name, condition=None):
        under(condition, self.copy(target, target, device, name).wait_recv)

    def finish(self):
        for copy, condition in self.sent:
            under(condition, copy.wait_send)


def greet(devices):
    barrier = pltpu.get_barrier_semaphore()
    for device in devices:
        pl.semaphore_signal(
            barrier, inc=1, device_id=device, device_id_type=pl.DeviceIdType.MESH
        )
    pl.semaphore_wait(barrier, len(devices))


def gather_kernel(count, *refs):
    heads_in, tokens_in = refs[:2]
    hidden_in = refs[2 : 2 + count]
    heads, tokens = refs[2 + count : 4 + count]
    hidden = refs[4 + count : 4 + 2 * count]
    send_sem, recv_sem, local_sem = refs[4 + 2 * count :]
    y, z, x, c = my_place()
    me = x * 2 + c
    chip = z * 2 + x
    chips = LINE * 2
    group = {d: device_at(y, z, (x + d[0]) % 2, (c + d[1]) % 2) for d in GROUP[1:]}
    plane = {d: device_at(y, along_line(z, d[0]), (x + d[1]) % 2, c) for d in PLANE}
    row_peer = device_at(1 - y, z, x, c)
    core_peer = group[(0, 1)]
    up = device_at(y, jnp.minimum(z + 1, LINE - 1), x, c)
    down = device_at(y, jnp.maximum(z - 1, 0), x, c)
    can_up = z < LINE - 1
    can_down = z > 0
    greet([row_peer, core_peer, group[(1, 1)]] + list(plane.values()))
    post = Courier(send_sem, recv_sem)

    def member(d):
        return ((x + d[0]) % 2) * 2 + (c + d[1]) % 2

    def chip_of(d):
        return along_line(z, d[0]) * 2 + (x + d[1]) % 2

    def columns(ref, which):
        width = ref.shape[1] // chips
        return ref.at[:, pl.ds(pl.multiple_of(which * width, 128), width)]

    for d, device in group.items():
        post.send(heads_in.at[member(d)], heads.at[y, z, me], device, ("group", d))
    local = [(heads_in.at[me], heads.at[y, z, me]), (tokens_in, tokens.at[0])]
    local += [(columns(w, chip), out.at[y, chip, c]) for w, out in zip(hidden_in, hidden)]
    kept = []
    for slot, (source, target) in enumerate(local):
        kept.append(pltpu.make_async_copy(source, target, local_sem.at[slot]))
        kept[-1].start()
    for d, device in group.items():
        post.send(tokens_in, tokens.at[d[0] * 2 + d[1]], device, ("tokens", d))

    def spread(source, which):
        target = heads.at[y, z, member(which)]
        post.send(source, target, up, ("up", 1, which), can_up)
        post.send(source, target, down, ("down", 1, which), can_down)
        post.send(source, target, row_peer, ("row", 0, 0, which))

    def plane_out(m):
        for d in PLANE:
            post.send(
                columns(hidden_in[m], chip_of(d)),
                hidden[m].at[y, chip, c],
                plane[d],
                ("plane", m, d),
            )
        own = columns(hidden_in[m], chip)
        post.send(own, hidden[m].at[y, chip, c], row_peer, ("far", m, (0, 0)))
        post.send(own, hidden[m].at[y, chip, c], core_peer, ("core", 0, m, (0, 0)))

    def plane_in(m):
        for d in PLANE:
            block = hidden[m].at[y, chip_of(d), c]
            post.arrive(block, core_peer, ("plane", m, d))
            post.send(block, block, row_peer, ("far", m, d))
            post.send(block, block, core_peer, ("core", 0, m, d))

    spread(heads_in.at[me], (0, 0))
    if count:
        plane_out(0)
    for d in GROUP[1:]:
        block = heads.at[y, z, member(d)]
        post.arrive(block, core_peer, ("group", d))
        spread(block, d)
    sides = ((-1, "up", up, can_up), (1, "down", down, can_down))
    for step in range(1, LINE):
        for d in GROUP:
            for sign, name, device, onward in sides:
                here = z >= step if sign < 0 else z <= LINE - 1 - step
                block = heads.at[y, jnp.clip(z + sign * step, 0, LINE - 1), member(d)]
                post.arrive(block, core_peer, (name, step, d), here)
                if step < LINE - 1:
                    post.send(block, block, device, (name, step + 1, d), here & onward)
                post.send(block, block, row_peer, ("row", sign, step, d), here)
        if step == 1 and count:
            plane_in(0)
            if count > 1:
                plane_out(1)
    for m in range(1, count):
        if m + 1 < count:
            plane_out(m + 1)
        plane_in(m)
    for m in range(count):
        for d in ((0, 0),) + PLANE:
            block = hidden[m].at[1 - y, chip_of(d), c]
            post.arrive(block, core_peer, ("far", m, d))
            post.send(block, block, core_peer, ("core", 1, m, d))
    for d in GROUP[1:]:
        post.arrive(tokens.at[d[0] * 2 + d[1]], core_peer, ("tokens", d))
    for d in GROUP:
        post.arrive(heads.at[1 - y, z, member(d)], core_peer, ("row", 0, 0, d))
        for step in range(1, LINE):
            for sign, name, device, onward in sides:
                here = z >= step if sign < 0 else z <= LINE - 1 - step
                block = heads.at[1 - y, jnp.clip(z + sign * step, 0, LINE - 1), member(d)]
                post.arrive(block, core_peer, ("row", sign, step, d), here)
    for m in range(count):
        for half in range(2):
            for d in ((0, 0),) + PLANE:
                block = hidden[m].at[y if half == 0 else 1 - y, chip_of(d), 1 - c]
                post.arrive(block, core_peer, ("core", half, m, d))
    post.finish()
    for copy in kept:
        copy.wait()


def gather_weights(heads_in, tokens_in, hidden_in):
    rows = heads_in.shape[1]
    count = len(hidden_in)
    anywhere = pl.BlockSpec(memory_space=pl.ANY)
    copies = 44 + 4 * len(GROUP) + (7 + 24) * count
    outs = [
        jax.ShapeDtypeStruct((2, LINE, 4, rows, heads_in.shape[2]), jnp.bfloat16),
        jax.ShapeDtypeStruct((4,) + tokens_in.shape, jnp.bfloat16),
    ]
    for matrix in hidden_in:
        width = matrix.shape[1] // (LINE * 2)
        outs.append(jax.ShapeDtypeStruct((2, LINE * 2, 2, rows, width), jnp.bfloat16))
    found = pl.pallas_call(
        functools.partial(gather_kernel, count),
        out_shape=outs,
        in_specs=[anywhere] * (2 + count),
        out_specs=[anywhere] * (2 + count),
        scratch_shapes=[
            pltpu.SemaphoreType.DMA((copies,)),
            pltpu.SemaphoreType.DMA((copies,)),
            pltpu.SemaphoreType.DMA((2 + count,)),
        ],
        compiler_params=pltpu.CompilerParams(collective_id=0, has_side_effects=True),
    )(heads_in, tokens_in, *hidden_in)
    total = 2 * LINE * 4 * rows
    heads = found[0].reshape(total, heads_in.shape[2])
    tokens = found[1].reshape(4 * tokens_in.shape[0], tokens_in.shape[1])
    return heads, tokens, [block.reshape(total, block.shape[-1]) for block in found[2:]]


def scatter_kernel(parts, count, *refs):
    heads_in = refs[:parts]
    hidden_in = refs[parts : parts + count]
    heads = refs[parts + count : 2 * parts + count]
    hidden = refs[2 * parts + count : 2 * (parts + count)]
    scratch = refs[2 * (parts + count) :]
    own, across, above, below = (scratch[n * parts : (n + 1) * parts] for n in range(4))
    send_sem, recv_sem, load_sem, head_send, head_recv, local_sem = scratch[4 * parts :]
    y, z, x, c = my_place()
    me = x * 2 + c
    chip = z * 2 + x
    chips = LINE * 2
    group = {d: device_at(y, z, (x + d[0]) % 2, (c + d[1]) % 2) for d in GROUP[1:]}
    plane = {d: device_at(y, along_line(z, d[0]), (x + d[1]) % 2, c) for d in PLANE}
    row_peer = device_at(1 - y, z, x, c)
    core_peer = group[(0, 1)]
    up = device_at(y, jnp.minimum(z + 1, LINE - 1), x, c)
    down = device_at(y, jnp.maximum(z - 1, 0), x, c)
    greet([row_peer, core_peer, group[(1, 1)]] + list(plane.values()))
    post = Courier(send_sem, recv_sem)

    def member(d):
        return ((x + d[0]) % 2) * 2 + (c + d[1]) % 2

    def chip_of(d):
        return along_line(z, d[0]) * 2 + (x + d[1]) % 2

    order = [(0, 0, None)]
    for step in range(1, LINE):
        order = [(1, step, z <= LINE - 1 - step), (-1, step, z >= step)] + order

    def head_copy(p, stage, source, target, device, place, m):
        return pltpu.make_async_remote_copy(
            src_ref=source,
            dst_ref=target,
            send_sem=head_send.at[p, stage, place, m],
            recv_sem=head_recv.at[p, stage, place, m],
            device_id=device,
            device_id_type=pl.DeviceIdType.MESH,
        )

    def to_row_copy(p, place, m):
        return head_copy(
            p, 0, heads_in[p].at[1 - y, place, m], across[p].at[place, m], row_peer, place, m
        )

    def load_copy(p, place, m):
        return pltpu.make_async_copy(
            heads_in[p].at[y, place, m], own[p].at[place, m], load_sem.at[p, place, m]
        )

    def up_copy(p, place, m):
        return head_copy(p, 1, own[p].at[place, m], below[p].at[place, m], up, place, m)

    def down_copy(p, place, m):
        return head_copy(p, 2, own[p].at[place, m], above[p].at[place, m], down, place, m)

    def each(action):
        lax.fori_loop(0, 4, lambda m, carry: (action(m), carry)[1], 0)

    for sign, step, okay in order:
        place = z + sign * step

        def start(m, place=place):
            for p in range(parts):
                to_row_copy(p, place, m).start()
                load_copy(p, place, m).start()

        under(okay, lambda start=start: each(start))
    kept = []
    for m in range(count):
        for d in PLANE:
            width = hidden[m].shape[1] // chips
            post.send(
                hidden_in[m].at[chip_of(d)],
                hidden[m].at[:, pl.ds(pl.multiple_of(chip * width, 128), width)],
                plane[d],
                ("plane", m, d),
            )
        kept.append(
            pltpu.make_async_copy(
                hidden_in[m].at[chip],
                hidden[m].at[:, pl.ds(pl.multiple_of(chip * width, 128), width)],
                local_sem.at[m],
            )
        )
        kept[-1].start()

    def ready(p, place, m):
        to_row_copy(p, place, m).wait_recv()
        load_copy(p, place, m).wait()
        return wide(own[p][place, m]) + wide(across[p][place, m])

    for sign, step, okay in order[:-1]:
        place = z + sign * step

        def relay(m, place=place, sign=sign):
            for p in range(parts):
                own[p][place, m] = low(ready(p, place, m))
            if sign > 0:
                @pl.when(z > 0)
                def _():
                    for p in range(parts):
                        up_copy(p, place, m).wait_recv()
                        own[p][place, m] = low(wide(own[p][place, m]) + wide(below[p][place, m]))
            else:
                @pl.when(z < LINE - 1)
                def _():
                    for p in range(parts):
                        down_copy(p, place, m).wait_recv()
                        own[p][place, m] = low(wide(own[p][place, m]) + wide(above[p][place, m]))
            for p in range(parts):
                (up_copy if sign > 0 else down_copy)(p, place, m).start()

        under(okay, lambda relay=relay: each(relay))

    def settle(m):
        for p in range(parts):
            own[p][z, m] = low(ready(p, z, m))

        @pl.when(z > 0)
        def _():
            for p in range(parts):
                up_copy(p, z, m).wait_recv()
                own[p][z, m] = low(wide(own[p][z, m]) + wide(below[p][z, m]))

        @pl.when(z < LINE - 1)
        def _():
            for p in range(parts):
                down_copy(p, z, m).wait_recv()
                own[p][z, m] = low(wide(own[p][z, m]) + wide(above[p][z, m]))

    each(settle)
    for p in range(parts):
        kept.append(pltpu.make_async_copy(own[p].at[z, me], heads[p].at[me], local_sem.at[count + p]))
        kept[-1].start()
        for d, device in group.items():
            post.send(own[p].at[z, member(d)], heads[p].at[me], device, ("group", p, d))
    for p in range(parts):
        for d in GROUP[1:]:
            post.arrive(heads[p].at[member(d)], core_peer, ("group", p, d))
    for m in range(count):
        for d in PLANE:
            width = hidden[m].shape[1] // chips
            block = hidden[m].at[:, pl.ds(pl.multiple_of(chip_of(d) * width, 128), width)]
            post.arrive(block, core_peer, ("plane", m, d))
    for sign, step, okay in order:
        place = z + sign * step

        def drain(m, place=place, sign=sign):
            for p in range(parts):
                to_row_copy(p, place, m).wait_send()
                if sign > 0:
                    up_copy(p, place, m).wait_send()
                if sign < 0:
                    down_copy(p, place, m).wait_send()

        under(okay, lambda drain=drain: each(drain))
    post.finish()
    for copy in kept:
        copy.wait()


def scatter_weights(head_sums, hidden_sums):
    parts, count = len(head_sums), len(hidden_sums)
    rows = head_sums[0].shape[0] // (2 * LINE * 4)
    anywhere = pl.BlockSpec(memory_space=pl.ANY)
    copies = 7 * count + 3 * parts
    outs = [jax.ShapeDtypeStruct((4, rows, h.shape[1]), jnp.bfloat16) for h in head_sums]
    outs += [
        jax.ShapeDtypeStruct((rows, h.shape[0] * h.shape[2]), jnp.bfloat16) for h in hidden_sums
    ]
    found = pl.pallas_call(
        functools.partial(scatter_kernel, parts, count),
        out_shape=outs,
        in_specs=[anywhere] * (parts + count),
        out_specs=[anywhere] * (parts + count),
        scratch_shapes=[
            pltpu.VMEM((LINE, 4, rows, h.shape[1]), jnp.bfloat16) for _ in range(4) for h in head_sums
        ]
        + [
            pltpu.SemaphoreType.DMA((copies,)),
            pltpu.SemaphoreType.DMA((copies,)),
            pltpu.SemaphoreType.DMA((parts, LINE, 4)),
            pltpu.SemaphoreType.DMA((parts, 3, LINE, 4)),
            pltpu.SemaphoreType.DMA((parts, 3, LINE, 4)),
            pltpu.SemaphoreType.DMA((count + parts,)),
        ],
        compiler_params=pltpu.CompilerParams(
            collective_id=1, has_side_effects=True, vmem_limit_bytes=40 << 20
        ),
    )(
        *[h.reshape(2, LINE, 4, rows, h.shape[1]) for h in head_sums],
        *hidden_sums,
    )
    return found[:parts], found[parts:]


def split_columns(matrix, count):
    rows, cols = matrix.shape
    return matrix.reshape(rows, count, cols // count).transpose(1, 0, 2)


def join_columns(blocks):
    count, rows, cols = blocks.shape
    return wide(blocks).transpose(1, 0, 2).reshape(rows, count * cols)


def turn(values, cosine, sine):
    half_dim = HEAD_DIM // 2
    front_half = values[..., :half_dim]
    back_half = values[..., half_dim:]
    return jnp.concatenate(
        [front_half * cosine - back_half * sine, back_half * cosine + front_half * sine], axis=-1
    )


def dot(left_side, right_side):
    return jnp.dot(left_side, right_side, preferred_element_type=jnp.float32)


def dot_rows(left_side, right_side):
    return jnp.einsum("tf,df->td", left_side, right_side, preferred_element_type=jnp.float32)


def outer_sum(left_side, right_side):
    return jnp.einsum("td,tf->df", left_side, right_side, preferred_element_type=jnp.float32)


def per_device_line(
    tokens,
    cotangent,
    doc_ids,
    bit_levels,
    w_query,
    w_key,
    w_value,
    w_proj,
    w_gate,
    w_up,
    w_down,
    gain_first,
    gain_second,
    gain_third,
    gain_fourth,
):
    spot = Spot()
    count = tokens.shape[1]
    group_size = HEADS // KV_HEADS
    query_width = HEADS * HEAD_DIM
    score_scale = HEAD_DIM ** (-0.5)
    span = 4 * count

    heads_in = low(
        jnp.concatenate(
            [
                split_columns(dequant(w_query, bit_levels[0], D, qk_boost), KV_HEADS),
                split_columns(dequant(w_key, bit_levels[1], D, qk_boost), KV_HEADS),
                split_columns(dequant(w_value, bit_levels[2], D, 1.0), KV_HEADS),
                split_columns(dequant(w_proj, bit_levels[3], query_width, 1.0), KV_HEADS),
            ],
            axis=2,
        )
    )
    flat_tokens = wide(tokens).reshape(count, D)
    normed_low = low(rmsnorm(flat_tokens, gain_first))
    all_heads, normed_all, (gate_w, up_w, down_w) = gather_weights(
        heads_in,
        normed_low,
        [
            low(dequant(w_gate, bit_levels[4], D, 1.0)),
            low(dequant(w_up, bit_levels[5], D, 1.0)),
            low(dequant(w_down, bit_levels[6], FF, 1.0)),
        ],
    )
    head_width = (group_size + 2) * HEAD_DIM
    heads_w = all_heads[:, :head_width]
    proj_w = all_heads[:, head_width:]

    inner = jnp.arange(count, dtype=jnp.int32)
    offsets = jnp.concatenate(
        [member(spot, dx, dc) * count + inner for dx in range(2) for dc in range(2)]
    )
    positions = spot.z * span + offsets
    half_dim = HEAD_DIM // 2
    frequency = 10000.0 ** (-(2.0 / HEAD_DIM) * jnp.arange(half_dim, dtype=jnp.float32))
    angles = positions.astype(jnp.float32)[:, None] * frequency[None, :]
    cosine = jnp.cos(angles)
    sine = jnp.sin(angles)
    docs = doc_ids.reshape(LINE, 2, 2, count)
    docs = jnp.where(spot.x == 1, docs[:, ::-1], docs)
    docs = jnp.where(spot.c == 1, docs[:, :, ::-1], docs).reshape(LINE, span)
    query_docs = pick(docs, spot.z)

    pre = dot(normed_all, heads_w)
    wide_q = group_size * HEAD_DIM
    query_rot = low(
        turn(
            pre[:, :wide_q].reshape(span, group_size, HEAD_DIM),
            cosine[:, None],
            sine[:, None],
        )
    )
    key_rot = low(turn(pre[:, wide_q : wide_q + HEAD_DIM], cosine, sine))
    value_low = low(pre[:, wide_q + HEAD_DIM :])
    key_value = [jnp.concatenate([key_rot, value_low], axis=1)]
    for _ in range(1, LINE):
        key_value.append(up_line(key_value[-1]))

    totals = 0.0
    summed = 0.0
    saved = []
    for back, block in enumerate(key_value):
        key_piece, value_piece = block[:, :HEAD_DIM], block[:, HEAD_DIM:]
        key_docs = pick(docs, jnp.maximum(spot.z - back, 0))
        key_pos = positions - back * span
        allowed = (
            (key_pos[None, :] <= positions[:, None])
            & (key_pos[None, :] >= 0)
            & (key_docs[None, :] == query_docs[:, None])
        )
        raw_scores = (
            jnp.einsum("qrd,kd->rqk", query_rot, key_piece, preferred_element_type=jnp.float32)
            * score_scale
        )
        bent = jnp.tanh(raw_scores / softcap)
        weights = jnp.where(allowed[None], jnp.exp(softcap * bent), 0.0)
        totals = totals + jnp.sum(weights, axis=-1)
        summed = summed + jnp.einsum(
            "rqk,kd->qrd", low(weights), value_piece, preferred_element_type=jnp.float32
        )
        saved.append((key_piece, value_piece, weights, bent))
    denominator = jnp.transpose(totals)[..., None]
    mixed_out = summed / denominator
    mixed_low = low(mixed_out).reshape(span, wide_q)
    attn_out = reduce_group(low(dot_rows(mixed_low, proj_w)).reshape(2, 2, count, D))
    hidden_one = flat_tokens + rmsnorm(attn_out, gain_second)
    mid_low = low(rmsnorm(hidden_one, gain_third))

    mid_chunks = gather_plane(spot, mid_low)
    gates, acts, ffn_chunks = [], [], []
    for chunk in mid_chunks:
        gate_pre = dot(chunk, gate_w)
        up_pre = dot(chunk, up_w)
        activated = low(gelu_product(gate_pre, up_pre))
        gates.append((gate_pre, up_pre))
        acts.append(activated)
        ffn_chunks.append(low(dot_rows(activated, down_w)).reshape(2, count, D))
    ffn_out = reduce_plane(lax.optimization_barrier(ffn_chunks))
    result = hidden_one + rmsnorm(ffn_out, gain_fourth)
    layer_out = low(result).reshape(1, count, D)

    upstream = wide(cotangent).reshape(count, D)
    grad_ffn, fourth_part = jax.vjp(rmsnorm, ffn_out, gain_fourth)[1](upstream)
    grad_chunks = gather_plane(spot, low(grad_ffn))
    gate_grads, up_grads, back_chunks = [], [], []
    for chunk, (gate_pre, up_pre) in zip(grad_chunks, gates):
        grad_act = dot(chunk, down_w)
        grad_gate_pre, grad_up_pre = jax.vjp(gelu_product, gate_pre, up_pre)[1](grad_act)
        gate_grads.append(low(grad_gate_pre))
        up_grads.append(low(grad_up_pre))
        back_chunks.append(
            low(dot_rows(gate_grads[-1], gate_w) + dot_rows(up_grads[-1], up_w)).reshape(
                2, count, D
            )
        )
    back_chunks, mid_chunks, gate_grads, up_grads, grad_chunks, acts = lax.optimization_barrier(
        (back_chunks, mid_chunks, gate_grads, up_grads, grad_chunks, acts)
    )
    grad_mid = reduce_plane(back_chunks)
    mid_all = jnp.concatenate(mid_chunks, axis=0)
    gate_sums = narrow_hidden(spot, low(outer_sum(mid_all, jnp.concatenate(gate_grads, axis=0))))
    up_sums = narrow_hidden(spot, low(outer_sum(mid_all, jnp.concatenate(up_grads, axis=0))))
    down_sums = narrow_hidden(
        spot,
        low(outer_sum(jnp.concatenate(grad_chunks, axis=0), jnp.concatenate(acts, axis=0))),
    )

    hidden_part, third_part = jax.vjp(rmsnorm, hidden_one, gain_third)[1](grad_mid)
    grad_hidden = upstream + hidden_part
    grad_attn, second_part = jax.vjp(rmsnorm, attn_out, gain_second)[1](grad_hidden)
    grad_attn_all = gather_group(low(grad_attn))
    proj_sums = low(outer_sum(grad_attn_all, mixed_low))

    grad_mixed = dot(grad_attn_all, proj_w).reshape(span, group_size, HEAD_DIM)
    grad_summed = low(grad_mixed / denominator)
    delta = jnp.transpose(jnp.sum(grad_mixed * mixed_out, axis=-1)) / totals
    grad_query_rot = 0.0
    passed = None
    for back in range(LINE - 1, -1, -1):
        key_piece, value_piece, weights, bent = saved[back]
        grad_weights = (
            jnp.einsum(
                "qrd,kd->rqk", grad_summed, value_piece, preferred_element_type=jnp.float32
            )
            - delta[..., None]
        )
        grad_raw = low(weights * grad_weights * (1.0 - bent * bent))
        grad_query_rot = grad_query_rot + jnp.einsum(
            "rqk,kd->qrd", grad_raw, key_piece, preferred_element_type=jnp.float32
        )
        key_term = (
            jnp.einsum("rqk,qrd->kd", grad_raw, query_rot, preferred_element_type=jnp.float32)
            * score_scale
        )
        value_term = jnp.einsum(
            "rqk,qrd->kd", low(weights), grad_summed, preferred_element_type=jnp.float32
        )
        sums = jnp.concatenate([key_term, value_term], axis=1)
        if passed is not None:
            sums = sums + wide(down_line(passed))
        passed = low(sums)
    grad_query_pre = low(
        turn(grad_query_rot * score_scale, cosine[:, None], -sine[:, None])
    ).reshape(span, wide_q)
    grad_key_pre = low(turn(sums[:, :HEAD_DIM], cosine, -sine))
    grad_pre = jnp.concatenate([grad_query_pre, grad_key_pre, low(sums[:, HEAD_DIM:])], axis=1)
    grad_shares = dot_rows(grad_pre, heads_w)
    first_part = jnp.sum(wide(normed_all) * grad_shares, axis=0) / (1.0 + gain_first)
    gain_sums = jnp.stack([first_part, second_part, third_part, fourth_part], axis=1)
    gain_sums = low(jnp.pad(gain_sums, ((0, 0), (0, 124))))
    (head_rows, proj_rows), (grad_gate, grad_up, grad_down) = scatter_weights(
        [
            low(outer_sum(normed_all, grad_pre)),
            jnp.concatenate([proj_sums, gain_sums], axis=1),
        ],
        [gate_sums, up_sums, down_sums],
    )
    grad_in = reduce_group(low(grad_shares).reshape(2, 2, count, D))
    tokens_part = jax.vjp(lambda v: rmsnorm(v, gain_first), flat_tokens)[1](grad_in)[0]
    grad_tokens = (grad_hidden + tokens_part).reshape(1, count, D)
    gains = jnp.sum(wide(proj_rows[:, :, wide_q:]), axis=0)
    return (
        layer_out,
        grad_tokens,
        join_columns(head_rows[:, :, :wide_q]),
        join_columns(head_rows[:, :, wide_q : wide_q + HEAD_DIM]),
        join_columns(head_rows[:, :, wide_q + HEAD_DIM :]),
        join_columns(proj_rows[:, :, :wide_q]),
        wide(grad_gate),
        wide(grad_up),
        wide(grad_down),
        gains[:, 0],
        gains[:, 1],
        gains[:, 2],
        gains[:, 3],
    )


def solution(mesh):
    placed = (
        P("rows", "seq", None),
        P("rows", "seq", None),
        P("rows", None),
        P(),
        P(("rows", "seq"), None),
        P(("rows", "seq"), None),
        P(("rows", "seq"), None),
        P(("rows", "seq"), None),
        P(("rows", "seq"), None),
        P(("rows", "seq"), None),
        P(("rows", "seq"), None),
        P(),
        P(),
        P(),
        P(),
    )
    sizes = dict(mesh.shape)
    fits = sizes["rows"] == 2 and sizes["seq"] == LINE * 4
    return jax.shard_map(
        per_device_line if fits else per_device_plain,
        mesh=mesh,
        in_specs=placed,
        out_specs=(
            P("rows", "seq", None),
            P("rows", "seq", None),
            P(("rows", "seq"), None),
            P(("rows", "seq"), None),
            P(("rows", "seq"), None),
            P(("rows", "seq"), None),
            P(("rows", "seq"), None),
            P(("rows", "seq"), None),
            P(("rows", "seq"), None),
            P(("rows", "seq")),
            P(("rows", "seq")),
            P(("rows", "seq")),
            P(("rows", "seq")),
        ),
        check_vma=False,
    )
```

```python
import functools
import math

import jax
import jax.numpy as jnp
from jax import lax
from jax.experimental import pallas as pl
from jax.experimental.pallas import tpu as pltpu
from jax.sharding import PartitionSpec as P

D = 2304
FF = 9216
HEADS = 8
KV_HEADS = 4
HEAD_DIM = 256


softcap = 50.0
epsilon = 1e-06
qk_boost = 1.65


def dequant(levels_int, level_idx, fan_in, boost):
    bits = jnp.where(level_idx == 0, 0, jnp.where(level_idx == 1, 4, 6)).astype(jnp.int32)
    middle = jnp.where(level_idx == 0, 0, jnp.where(level_idx == 1, 8, 32)).astype(jnp.int32)
    sliced = ((levels_int >> bits) << bits) + middle
    return sliced.astype(jnp.float32) * (boost / (74.0 * math.sqrt(fan_in)))


def rmsnorm(values, gain_vec):
    return (
        values
        * lax.rsqrt(jnp.mean(values * values, axis=-1, keepdims=True) + epsilon)
        * (1.0 + gain_vec)
    )


def rotate(values, positions, direction):
    half_dim = HEAD_DIM // 2
    frequency = 10000.0 ** (-(2.0 / HEAD_DIM) * jnp.arange(half_dim, dtype=jnp.float32))
    angles = positions.astype(jnp.float32)[:, None] * frequency[None, :]
    cosine = jnp.cos(angles)[:, None, :]
    sine = jnp.sin(angles)[:, None, :] * direction
    front_half = values[..., :half_dim]
    back_half = values[..., half_dim:]
    return jnp.concatenate(
        [front_half * cosine - back_half * sine, back_half * cosine + front_half * sine], axis=-1
    )


def gelu_product(gate_vals, up_vals):
    return jax.nn.gelu(gate_vals, approximate=True) * up_vals


def per_device_plain(
    tokens,
    cotangent,
    doc_ids,
    bit_levels,
    w_query,
    w_key,
    w_value,
    w_proj,
    w_gate,
    w_up,
    w_down,
    gain_first,
    gain_second,
    gain_third,
    gain_fourth,
):
    rows_here = tokens.shape[0]
    seq_block = tokens.shape[1]
    token_count = rows_here * seq_block
    local_rows = w_query.shape[0]
    group_size = HEADS // KV_HEADS
    query_width = HEADS * HEAD_DIM
    key_width = KV_HEADS * HEAD_DIM
    score_scale = HEAD_DIM ** (-0.5)
    offset = lax.axis_index("seq") * seq_block
    positions = offset + jnp.arange(seq_block, dtype=jnp.int32)
    query_docs = lax.dynamic_slice_in_dim(doc_ids, offset, seq_block, 1)
    query_local = dequant(w_query, bit_levels[0], D, qk_boost).astype(jnp.bfloat16)
    key_local = dequant(w_key, bit_levels[1], D, qk_boost).astype(jnp.bfloat16)
    value_local = dequant(w_value, bit_levels[2], D, 1.0).astype(jnp.bfloat16)
    proj_local = dequant(w_proj, bit_levels[3], query_width, 1.0).astype(jnp.bfloat16)
    gate_local = dequant(w_gate, bit_levels[4], D, 1.0).astype(jnp.bfloat16)
    up_local = dequant(w_up, bit_levels[5], D, 1.0).astype(jnp.bfloat16)
    down_local = dequant(w_down, bit_levels[6], FF, 1.0).astype(jnp.bfloat16)
    query_full, key_full, value_full, proj_full = (
        lax.all_gather(query_local, ("rows", "seq"), axis=0, tiled=True),
        lax.all_gather(key_local, ("rows", "seq"), axis=0, tiled=True),
        lax.all_gather(value_local, ("rows", "seq"), axis=0, tiled=True),
        lax.all_gather(proj_local, ("rows", "seq"), axis=0, tiled=True),
    )
    row_groups = lax.axis_size("rows")
    seq_count = lax.axis_size("seq")
    col_width = FF // seq_count
    stacked = jnp.stack([gate_local, up_local, down_local]).reshape(
        3, local_rows, seq_count, col_width
    )
    spread = jnp.concatenate([stacked] * row_groups, axis=2)
    columns_all = lax.all_to_all(
        spread, ("rows", "seq"), split_axis=2, concat_axis=1, tiled=True
    ).reshape(3, D, col_width)
    gate_cols = columns_all[0]
    up_cols = columns_all[1]
    down_cols = columns_all[2]
    flat_tokens = tokens.astype(jnp.float32).reshape(token_count, D)
    normed_low = rmsnorm(flat_tokens, gain_first).astype(jnp.bfloat16)
    query_pre = jnp.dot(normed_low, query_full, preferred_element_type=jnp.float32)
    key_pre = jnp.dot(normed_low, key_full, preferred_element_type=jnp.float32)
    value_low = (
        jnp.dot(normed_low, value_full, preferred_element_type=jnp.float32)
        .astype(jnp.bfloat16)
        .reshape(rows_here, seq_block, KV_HEADS, HEAD_DIM)
    )
    query_rot = (
        rotate(query_pre.reshape(rows_here, seq_block, HEADS, HEAD_DIM), positions, 1.0)
        .astype(jnp.bfloat16)
        .reshape(rows_here, seq_block, KV_HEADS, group_size, HEAD_DIM)
    )
    key_rot = rotate(
        key_pre.reshape(rows_here, seq_block, KV_HEADS, HEAD_DIM), positions, 1.0
    ).astype(jnp.bfloat16)

    def piece_weights(key_piece):
        key_count = key_piece.shape[1]
        key_pos = jnp.arange(key_count, dtype=jnp.int32)
        raw_scores = (
            jnp.einsum(
                "bqgrd,bkgd->bgrqk", query_rot, key_piece, preferred_element_type=jnp.float32
            )
            * score_scale
        )
        allowed = (key_pos[None, :] <= positions[:, None])[None] & (
            doc_ids[:, None, :] == query_docs[:, :, None]
        )
        bent_score = jnp.tanh(raw_scores / softcap)
        weights = jnp.where(allowed[:, None, None], jnp.exp(softcap * bent_score), 0.0)
        return (weights, bent_score)

    key_piece = lax.all_gather(key_rot, "seq", axis=1, tiled=True)
    value_piece = lax.all_gather(value_low, "seq", axis=1, tiled=True)
    weights, bent_score = piece_weights(key_piece)
    summed = jnp.einsum(
        "bgrqk,bkgd->bqgrd",
        weights.astype(jnp.bfloat16),
        value_piece,
        preferred_element_type=jnp.float32,
    )
    totals, summed = (jnp.sum(weights, axis=-1), summed)
    denominator = jnp.transpose(totals, (0, 3, 1, 2))[..., None]
    mixed_out = summed / denominator
    mixed_low = mixed_out.astype(jnp.bfloat16).reshape(token_count, query_width)
    attn_out = jnp.einsum("th,dh->td", mixed_low, proj_full, preferred_element_type=jnp.float32)
    hidden_one = flat_tokens + rmsnorm(attn_out, gain_second)
    mid_low = rmsnorm(hidden_one, gain_third).astype(jnp.bfloat16)
    mid_row = lax.all_gather(mid_low.reshape(rows_here, seq_block, D), "seq", axis=1, tiled=True)
    gate_pre = jnp.einsum("btd,df->btf", mid_row, gate_cols, preferred_element_type=jnp.float32)
    up_pre = jnp.einsum("btd,df->btf", mid_row, up_cols, preferred_element_type=jnp.float32)
    activated = gelu_product(gate_pre, up_pre).astype(jnp.bfloat16)
    ffn_terms = jnp.einsum("btf,df->btd", activated, down_cols, preferred_element_type=jnp.float32)
    ffn_out = lax.psum_scatter(ffn_terms, "seq", scatter_dimension=1, tiled=True).reshape(
        token_count, D
    )
    result = hidden_one + rmsnorm(ffn_out, gain_fourth)
    layer_out = result.astype(jnp.bfloat16).reshape(rows_here, seq_block, D)
    upstream = cotangent.astype(jnp.float32).reshape(token_count, D)
    grad_ffn, fourth_part = jax.vjp(rmsnorm, ffn_out, gain_fourth)[1](upstream)
    grad_ffn_low = grad_ffn.astype(jnp.bfloat16)
    grad_row = lax.all_gather(
        grad_ffn_low.reshape(rows_here, seq_block, D), "seq", axis=1, tiled=True
    )
    grad_act = jnp.einsum("btd,df->btf", grad_row, down_cols, preferred_element_type=jnp.float32)
    grad_gate_pre, grad_up_pre = jax.vjp(gelu_product, gate_pre, up_pre)[1](grad_act)
    grad_gate_low = grad_gate_pre.astype(jnp.bfloat16)
    grad_up_low = grad_up_pre.astype(jnp.bfloat16)
    mid_terms = jnp.einsum(
        "btf,df->btd", grad_gate_low, gate_cols, preferred_element_type=jnp.float32
    ) + jnp.einsum("btf,df->btd", grad_up_low, up_cols, preferred_element_type=jnp.float32)
    grad_mid = lax.psum_scatter(mid_terms, "seq", scatter_dimension=1, tiled=True).reshape(
        token_count, D
    )
    column_terms = jnp.stack(
        [
            jnp.einsum("btd,btf->df", mid_row, grad_gate_low, preferred_element_type=jnp.float32),
            jnp.einsum("btd,btf->df", mid_row, grad_up_low, preferred_element_type=jnp.float32),
            jnp.einsum("btd,btf->df", grad_row, activated, preferred_element_type=jnp.float32),
        ]
    )
    returned = lax.all_to_all(
        column_terms.reshape(3, D, 1, col_width).astype(jnp.bfloat16),
        ("rows", "seq"),
        split_axis=1,
        concat_axis=2,
        tiled=True,
    ).astype(jnp.float32)
    column_sums = jnp.sum(
        returned.reshape(3, local_rows, row_groups, seq_count, col_width), axis=2
    ).reshape(3, local_rows, FF)
    hidden_part, third_part = jax.vjp(rmsnorm, hidden_one, gain_third)[1](grad_mid)
    grad_hidden = upstream + hidden_part
    grad_attn, second_part = jax.vjp(rmsnorm, attn_out, gain_second)[1](grad_hidden)
    grad_attn_low = grad_attn.astype(jnp.bfloat16)
    query_back, key_back, value_back, proj_back = (
        lax.all_gather(query_local, ("rows", "seq"), axis=0, tiled=True),
        lax.all_gather(key_local, ("rows", "seq"), axis=0, tiled=True),
        lax.all_gather(value_local, ("rows", "seq"), axis=0, tiled=True),
        lax.all_gather(proj_local, ("rows", "seq"), axis=0, tiled=True),
    )
    grad_mixed = jnp.dot(grad_attn_low, proj_back, preferred_element_type=jnp.float32).reshape(
        rows_here, seq_block, KV_HEADS, group_size, HEAD_DIM
    )
    grad_summed = (grad_mixed / denominator).astype(jnp.bfloat16)
    delta_rows = jnp.transpose(
        jnp.sum(grad_mixed * mixed_out, axis=-1) / denominator[..., 0], (0, 2, 3, 1)
    )
    key_piece = lax.all_gather(key_rot, "seq", axis=1, tiled=True)
    value_piece = lax.all_gather(value_low, "seq", axis=1, tiled=True)
    key_count = key_piece.shape[1]
    weights, bent_score = piece_weights(key_piece)
    grad_weights = (
        jnp.einsum(
            "bqgrd,bkgd->bgrqk", grad_summed, value_piece, preferred_element_type=jnp.float32
        )
        - delta_rows[..., None]
    )
    grad_raw = (weights * grad_weights * (1.0 - bent_score * bent_score)).astype(jnp.bfloat16)
    grad_queries = (
        jnp.einsum("bgrqk,bkgd->bqgrd", grad_raw, key_piece, preferred_element_type=jnp.float32)
        * score_scale
    )
    key_term = (
        jnp.einsum("bgrqk,bqgrd->bkgd", grad_raw, query_rot, preferred_element_type=jnp.float32)
        * score_scale
    )
    value_term = jnp.einsum(
        "bgrqk,bqgrd->bkgd",
        weights.astype(jnp.bfloat16),
        grad_summed,
        preferred_element_type=jnp.float32,
    )
    key_sums = key_term
    value_sums = value_term
    grad_query_rot, key_sums, value_sums = (grad_queries, key_sums, value_sums)
    grad_key_rot, grad_value_sum = (
        lax.psum_scatter(key_sums, "seq", scatter_dimension=1, tiled=True),
        lax.psum_scatter(value_sums, "seq", scatter_dimension=1, tiled=True),
    )
    grad_query_pre = (
        rotate(grad_query_rot.reshape(rows_here, seq_block, HEADS, HEAD_DIM), positions, -1.0)
        .astype(jnp.bfloat16)
        .reshape(token_count, query_width)
    )
    grad_key_pre = (
        rotate(grad_key_rot, positions, -1.0).astype(jnp.bfloat16).reshape(token_count, key_width)
    )
    grad_value_low = grad_value_sum.astype(jnp.bfloat16).reshape(token_count, key_width)
    grad_in = (
        jnp.einsum("tf,df->td", grad_query_pre, query_back, preferred_element_type=jnp.float32)
        + jnp.einsum("tf,df->td", grad_key_pre, key_back, preferred_element_type=jnp.float32)
        + jnp.einsum("tf,df->td", grad_value_low, value_back, preferred_element_type=jnp.float32)
    )
    tokens_part, first_part = jax.vjp(rmsnorm, flat_tokens, gain_first)[1](grad_in)
    grad_tokens = (grad_hidden + tokens_part).reshape(rows_here, seq_block, D)

    def outer_sum(left_side, right_side):
        return jnp.einsum("td,tf->df", left_side, right_side, preferred_element_type=jnp.float32)

    gain_terms = jnp.stack([first_part, second_part, third_part, fourth_part], axis=1)
    padding = jnp.zeros((D, 124), jnp.float32)
    weight_terms = jnp.concatenate(
        [
            outer_sum(normed_low, grad_query_pre),
            outer_sum(normed_low, grad_key_pre),
            outer_sum(normed_low, grad_value_low),
            outer_sum(grad_attn_low, mixed_low),
            gain_terms,
            padding,
        ],
        axis=1,
    )
    summed_terms = lax.psum_scatter(weight_terms, ("rows", "seq"), scatter_dimension=0, tiled=True)
    widths = [query_width, key_width, key_width, query_width]
    pieces_out = []
    column = 0
    for span_cols in widths:
        pieces_out.append(summed_terms[:, column : column + span_cols])
        column = column + span_cols
    return (
        layer_out,
        grad_tokens,
        pieces_out[0],
        pieces_out[1],
        pieces_out[2],
        pieces_out[3],
        column_sums[0],
        column_sums[1],
        column_sums[2],
        summed_terms[:, column],
        summed_terms[:, column + 1],
        summed_terms[:, column + 2],
        summed_terms[:, column + 3],
    )


AXES = ("rows", "seq")
LINE = 4


def moves(places, rule):
    found = []
    for index in range(places):
        y, rest = divmod(index, LINE * 4)
        z, x, c = rest // 4, (rest // 2) % 2, rest % 2
        target = rule(y, z, x, c)
        if target is not None:
            y_to, z_to, x_to, c_to = target
            found.append((index, y_to * LINE * 4 + (z_to * 2 + x_to) * 2 + c_to))
    return found


def send(value, rule):
    return lax.ppermute(value, AXES, moves(2 * LINE * 4, rule))


def to_row(value):
    return send(value, lambda y, z, x, c: (1 - y, z, x, c))


def to_x(value):
    return send(value, lambda y, z, x, c: (y, z, 1 - x, c))


def to_core(value):
    return send(value, lambda y, z, x, c: (y, z, x, 1 - c))


def to_pair(value):
    return send(value, lambda y, z, x, c: (y, z ^ 1, x, c))


def across_middle(value):
    return send(value, lambda y, z, x, c: (y, 3 - z, x, c) if z in (1, 2) else None)


def to_ends(value):
    return send(value, lambda y, z, x, c: (y, z ^ 1, x, c) if z in (1, 2) else None)


def from_ends(value):
    return send(value, lambda y, z, x, c: (y, z ^ 1, x, c) if z in (0, 3) else None)


def up_line(value):
    return send(value, lambda y, z, x, c: (y, z + 1, x, c) if z < LINE - 1 else None)


def down_line(value):
    return send(value, lambda y, z, x, c: (y, z - 1, x, c) if z > 0 else None)


def to_chip(value, dz, dx):
    return send(value, lambda y, z, x, c: (y, z ^ dz, x ^ dx, c))


def low(value):
    return value.astype(jnp.bfloat16)


def wide(value):
    return value.astype(jnp.float32)


def pick(array, index, axis=0):
    return lax.dynamic_index_in_dim(array, index, axis, keepdims=False)


def place(array, piece, starts):
    return lax.dynamic_update_slice(array, piece, starts)


class Spot:
    def __init__(self):
        self.y = lax.axis_index("rows")
        index = lax.axis_index("seq")
        self.z = index // 4
        self.x = (index // 2) % 2
        self.c = index % 2
        self.middle = (self.z == 1) | (self.z == 2)
        upper = self.z >= 2
        self.slots = [
            self.z,
            self.z ^ 1,
            jnp.where(upper, 1, 2).astype(jnp.int32),
            jnp.where(upper, 0, 3).astype(jnp.int32),
        ]


def gather_line(spot, own):
    pair = to_pair(own)
    near = across_middle(own)
    far = across_middle(pair)
    near_end = to_ends(near)
    far_end = to_ends(far)
    return [
        own,
        pair,
        jnp.where(spot.middle, near, near_end),
        jnp.where(spot.middle, far, far_end),
    ]


def reduce_line(parts):
    far = parts[3] + wide(from_ends(low(parts[3])))
    near = parts[2] + wide(from_ends(low(parts[2])))
    pair = parts[1] + wide(across_middle(low(far)))
    own = parts[0] + wide(across_middle(low(near)))
    return own + wide(to_pair(low(pair)))


def gather_group(own):
    over_x = to_x(own)
    return jnp.concatenate([own, to_core(own), over_x, to_core(over_x)], axis=0)


def reduce_group(parts):
    both = wide(parts[:, 0]) + wide(to_core(parts[:, 1]))
    return both[0] + wide(to_x(low(both[1])))


def gather_plane(spot, own):
    return [
        jnp.concatenate([block, to_row(block)], axis=0) for block in gather_line(spot, own)
    ]


def reduce_plane(chunks):
    parts = [None] * LINE
    for slot in (3, 2, 1, 0):
        if slot == 1:
            parts[3], chunks[1], chunks[0] = lax.optimization_barrier(
                (parts[3], chunks[1], chunks[0])
            )
        parts[slot] = wide(chunks[slot][0]) + wide(to_row(chunks[slot][1]))
    return reduce_line(parts)


def member(spot, dx, dc):
    return (spot.x ^ dx) * 2 + (spot.c ^ dc)


GROUP = ((0, 0), (0, 1), (1, 0), (1, 1))
PLANE = ((2, 0), (1, 0), (3, 0), (0, 1), (2, 1), (1, 1), (3, 1))
PLANE_FAR = ((2, 0), (3, 0), (2, 1), (3, 1), (1, 0), (1, 1), (0, 1))


def my_place():
    index = lax.axis_index("seq")
    return lax.axis_index("rows"), index // 4, (index // 2) % 2, index % 2


def along_line(z, step):
    return (z, z + 1 - 2 * (z % 2), (z + 2) % LINE, LINE - 1 - z)[step]


def device_at(y, z, x, c):
    return (y, (z * 2 + x) * 2 + c)


def under(condition, action):
    if condition is None:
        action()
    else:
        pl.when(condition)(action)


class Courier:
    def __init__(self, send_sem, recv_sem):
        self.send_sem = send_sem
        self.recv_sem = recv_sem
        self.names = {}
        self.sent = []

    def copy(self, source, target, device, name):
        slot = self.names.setdefault(name, len(self.names))
        return pltpu.make_async_remote_copy(
            src_ref=source,
            dst_ref=target,
            send_sem=self.send_sem.at[slot],
            recv_sem=self.recv_sem.at[slot],
            device_id=device,
            device_id_type=pl.DeviceIdType.MESH,
        )

    def send(self, source, target, device, name, condition=None):
        copy = self.copy(source, target, device, name)
        under(condition, copy.start)
        self.sent.append((copy, condition))

    def arrive(self, target, device, name, condition=None):
        under(condition, self.copy(target, target, device, name).wait_recv)

    def finish(self):
        for copy, condition in self.sent:
            under(condition, copy.wait_send)


def greet(devices):
    barrier = pltpu.get_barrier_semaphore()
    for device in devices:
        pl.semaphore_signal(
            barrier, inc=1, device_id=device, device_id_type=pl.DeviceIdType.MESH
        )
    pl.semaphore_wait(barrier, len(devices))


def gather_kernel(count, *refs):
    heads_in, tokens_in = refs[:2]
    hidden_in = refs[2 : 2 + count]
    heads, tokens = refs[2 + count : 4 + count]
    hidden = refs[4 + count : 4 + 2 * count]
    send_sem, recv_sem, local_sem = refs[4 + 2 * count :]
    y, z, x, c = my_place()
    me = x * 2 + c
    chip = z * 2 + y
    chips = LINE * 2
    group = {d: device_at(y, z, (x + d[0]) % 2, (c + d[1]) % 2) for d in GROUP[1:]}
    plane = {d: device_at((y + d[1]) % 2, along_line(z, d[0]), x, c) for d in PLANE}
    row_peer = device_at(1 - y, z, x, c)
    core_peer = group[(0, 1)]
    chip_peer = group[(1, 0)]
    up = device_at(y, jnp.minimum(z + 1, LINE - 1), x, c)
    down = device_at(y, jnp.maximum(z - 1, 0), x, c)
    can_up = z < LINE - 1
    can_down = z > 0
    greet(list(group.values()) + list(plane.values()))
    post = Courier(send_sem, recv_sem)

    def member(d):
        return ((x + d[0]) % 2) * 2 + (c + d[1]) % 2

    def chip_of(d):
        return along_line(z, d[0]) * 2 + (y + d[1]) % 2

    def columns(ref, which):
        width = ref.shape[1] // chips
        return ref.at[:, pl.ds(pl.multiple_of(which * width, 128), width)]

    for d, device in group.items():
        post.send(heads_in.at[member(d)], heads.at[y, z, me], device, ("group", d))
    local = [(heads_in.at[me], heads.at[y, z, me]), (tokens_in, tokens.at[0])]
    local += [(columns(w, chip), out.at[y, z, x, c]) for w, out in zip(hidden_in, hidden)]
    kept = []
    for slot, (source, target) in enumerate(local):
        kept.append(pltpu.make_async_copy(source, target, local_sem.at[slot]))
        kept[-1].start()
    for d, device in group.items():
        post.send(tokens_in, tokens.at[d[0] * 2 + d[1]], device, ("tokens", d))

    def spread(source, which):
        target = heads.at[y, z, member(which)]
        post.send(source, target, up, ("up", 1, which), can_up)
        post.send(source, target, down, ("down", 1, which), can_down)
        post.send(source, target, row_peer, ("row", 0, 0, which))

    def plane_out(m):
        for d in PLANE:
            post.send(
                columns(hidden_in[m], chip_of(d)),
                hidden[m].at[y, z, x, c],
                plane[d],
                ("plane", m, d),
            )
        own = columns(hidden_in[m], chip)
        post.send(own, hidden[m].at[y, z, x, c], chip_peer, ("far", m, (0, 0)))
        post.send(own, hidden[m].at[y, z, x, c], core_peer, ("core", 0, m, (0, 0)))

    def rows_of(m, d, x_from, c_from):
        return hidden[m].at[(y + d[1]) % 2, along_line(z, d[0]), x_from, c_from]

    def plane_in(m):
        for d in PLANE:
            block = rows_of(m, d, x, c)
            post.arrive(block, core_peer, ("plane", m, d))
            post.send(block, block, chip_peer, ("far", m, d))
            post.send(block, block, core_peer, ("core", 0, m, d))

    spread(heads_in.at[me], (0, 0))
    if count:
        plane_out(0)
    for d in GROUP[1:]:
        block = heads.at[y, z, member(d)]
        post.arrive(block, core_peer, ("group", d))
        spread(block, d)
    sides = ((-1, "up", up, can_up), (1, "down", down, can_down))
    for step in range(1, LINE):
        for d in GROUP:
            for sign, name, device, onward in sides:
                here = z >= step if sign < 0 else z <= LINE - 1 - step
                block = heads.at[y, jnp.clip(z + sign * step, 0, LINE - 1), member(d)]
                post.arrive(block, core_peer, (name, step, d), here)
                if step < LINE - 1:
                    post.send(block, block, device, (name, step + 1, d), here & onward)
                post.send(block, block, row_peer, ("row", sign, step, d), here)
        if step == 1 and count:
            plane_in(0)
            if count > 1:
                plane_out(1)
    for m in range(1, count):
        if m + 1 < count:
            plane_out(m + 1)
        plane_in(m)
    for m in range(count):
        for d in ((0, 0),) + PLANE:
            block = rows_of(m, d, 1 - x, c)
            post.arrive(block, core_peer, ("far", m, d))
            post.send(block, block, core_peer, ("core", 1, m, d))
    for d in GROUP[1:]:
        post.arrive(tokens.at[d[0] * 2 + d[1]], core_peer, ("tokens", d))
    for d in GROUP:
        post.arrive(heads.at[1 - y, z, member(d)], core_peer, ("row", 0, 0, d))
        for step in range(1, LINE):
            for sign, name, device, onward in sides:
                here = z >= step if sign < 0 else z <= LINE - 1 - step
                block = heads.at[1 - y, jnp.clip(z + sign * step, 0, LINE - 1), member(d)]
                post.arrive(block, core_peer, ("row", sign, step, d), here)
    for m in range(count):
        for half in range(2):
            for d in ((0, 0),) + PLANE:
                block = rows_of(m, d, x if half == 0 else 1 - x, 1 - c)
                post.arrive(block, core_peer, ("core", half, m, d))
    post.finish()
    for copy in kept:
        copy.wait()


def gather_weights(heads_in, tokens_in, hidden_in):
    rows = heads_in.shape[1]
    count = len(hidden_in)
    anywhere = pl.BlockSpec(memory_space=pl.ANY)
    copies = 44 + 4 * len(GROUP) + (7 + 24) * count
    outs = [
        jax.ShapeDtypeStruct((2, LINE, 4, rows, heads_in.shape[2]), jnp.bfloat16),
        jax.ShapeDtypeStruct((4,) + tokens_in.shape, jnp.bfloat16),
    ]
    for matrix in hidden_in:
        width = matrix.shape[1] // (LINE * 2)
        outs.append(jax.ShapeDtypeStruct((2, LINE, 2, 2, rows, width), jnp.bfloat16))
    found = pl.pallas_call(
        functools.partial(gather_kernel, count),
        out_shape=outs,
        in_specs=[anywhere] * (2 + count),
        out_specs=[anywhere] * (2 + count),
        scratch_shapes=[
            pltpu.SemaphoreType.DMA((copies,)),
            pltpu.SemaphoreType.DMA((copies,)),
            pltpu.SemaphoreType.DMA((2 + count,)),
        ],
        compiler_params=pltpu.CompilerParams(collective_id=0, has_side_effects=True),
    )(heads_in, tokens_in, *hidden_in)
    total = 2 * LINE * 4 * rows
    heads = found[0].reshape(total, heads_in.shape[2])
    tokens = found[1].reshape(4 * tokens_in.shape[0], tokens_in.shape[1])
    return heads, tokens, [block.reshape(total, block.shape[-1]) for block in found[2:]]


def scatter_kernel(parts, count, *refs):
    heads_in = refs[:parts]
    hidden_in = refs[parts : parts + count]
    heads = refs[parts + count : 2 * parts + count]
    hidden = refs[2 * parts + count : 2 * (parts + count)]
    scratch = refs[2 * (parts + count) :]
    own, across, above, below = (scratch[n * parts : (n + 1) * parts] for n in range(4))
    share, other_core, other_chip = scratch[4 * parts : 4 * parts + 3]
    send_sem, recv_sem, load_sem, head_send, head_recv, local_sem = scratch[4 * parts + 3 :]
    y, z, x, c = my_place()
    me = x * 2 + c
    chip = z * 2 + y
    chips = LINE * 2
    group = {d: device_at(y, z, (x + d[0]) % 2, (c + d[1]) % 2) for d in GROUP[1:]}
    plane = {d: device_at((y + d[1]) % 2, along_line(z, d[0]), x, c) for d in PLANE}
    row_peer = device_at(1 - y, z, x, c)
    core_peer = group[(0, 1)]
    chip_peer = group[(1, 0)]
    up = device_at(y, jnp.minimum(z + 1, LINE - 1), x, c)
    down = device_at(y, jnp.maximum(z - 1, 0), x, c)
    greet(list(group.values()) + list(plane.values()))
    post = Courier(send_sem, recv_sem)
    everyone = PLANE_FAR + ((0, 0),)

    def member(d):
        return ((x + d[0]) % 2) * 2 + (c + d[1]) % 2

    def owner(d):
        return (y + d[1]) % 2, along_line(z, d[0])

    order = [(0, 0, None)]
    for step in range(1, LINE):
        order = [(1, step, z <= LINE - 1 - step), (-1, step, z >= step)] + order

    def head_copy(p, stage, source, target, device, place, m):
        return pltpu.make_async_remote_copy(
            src_ref=source,
            dst_ref=target,
            send_sem=head_send.at[p, stage, place, m],
            recv_sem=head_recv.at[p, stage, place, m],
            device_id=device,
            device_id_type=pl.DeviceIdType.MESH,
        )

    def to_row_copy(p, place, m):
        return head_copy(
            p, 0, heads_in[p].at[1 - y, place, m], across[p].at[place, m], row_peer, place, m
        )

    def load_copy(p, place, m):
        return pltpu.make_async_copy(
            heads_in[p].at[y, place, m], own[p].at[place, m], load_sem.at[p, place, m]
        )

    def up_copy(p, place, m):
        return head_copy(p, 1, own[p].at[place, m], below[p].at[place, m], up, place, m)

    def down_copy(p, place, m):
        return head_copy(p, 2, own[p].at[place, m], above[p].at[place, m], down, place, m)

    def each(action):
        lax.fori_loop(0, 4, lambda m, carry: (action(m), carry)[1], 0)

    for sign, step, okay in order:
        place = z + sign * step

        def start(m, place=place):
            for p in range(parts):
                to_row_copy(p, place, m).start()
                load_copy(p, place, m).start()

        under(okay, lambda start=start: each(start))
    kept = []
    loads = {}
    for d in everyone:
        y_to, z_to = owner(d)
        for m in range(count):
            for side, x_to in ((0, 1 - x), (1, x)):
                post.send(
                    hidden_in[m].at[y_to, z_to, x_to, 1 - c],
                    other_core.at[m, y_to, z_to, x_to],
                    core_peer,
                    ("core", m, d, side),
                )
                loads[m, d, side] = pltpu.make_async_copy(
                    hidden_in[m].at[y_to, z_to, x_to, c],
                    share.at[m, y_to, z_to, x_to],
                    local_sem.at[count + parts + len(loads)],
                )
                loads[m, d, side].start()

    def add_up(target, terms):
        rows, width = target.shape

        def add(k, carry):
            lanes = pl.ds(pl.multiple_of(k * 128, 128), 128)
            total = wide(target[:, lanes])
            for term in terms:
                total = total + wide(term[:, lanes])
            target[:, lanes] = low(total)
            return carry

        lax.fori_loop(0, width // 128, add, 0)

    def over_chip(d):
        y_to, z_to = owner(d)
        for m in range(count):
            block = share.at[m, y_to, z_to, 1 - x]
            arrived = other_core.at[m, y_to, z_to, 1 - x]
            loads[m, d, 0].wait()
            post.arrive(arrived, core_peer, ("core", m, d, 0))
            add_up(block, [arrived])
            post.send(block, other_chip.at[m, y_to, z_to], chip_peer, ("chip", m, d))

    def landing(m, which):
        width = hidden[m].shape[1] // chips
        return hidden[m].at[:, pl.ds(pl.multiple_of(which * width, 128), width)]

    def over_plane(d):
        y_to, z_to = owner(d)
        for m in range(count):
            block = share.at[m, y_to, z_to, x]
            loads[m, d, 1].wait()
            post.arrive(other_core.at[m, y_to, z_to, x], core_peer, ("core", m, d, 1))
            post.arrive(other_chip.at[m, y_to, z_to], core_peer, ("chip", m, d))
            add_up(block, [other_core.at[m, y_to, z_to, x], other_chip.at[m, y_to, z_to]])
            if d == (0, 0):
                kept.append(pltpu.make_async_copy(block, landing(m, chip), local_sem.at[m]))
                kept[-1].start()
            else:
                post.send(block, landing(m, chip), plane[d], ("plane", m, d))

    for d in everyone:
        over_chip(d)

    def ready(p, place, m):
        to_row_copy(p, place, m).wait_recv()
        load_copy(p, place, m).wait()
        return wide(own[p][place, m]) + wide(across[p][place, m])

    planned = [everyone[:1], everyone[1:2], everyone[2:3], everyone[3:4], everyone[4:6], everyone[6:]]
    for (sign, step, okay), hidden_now in zip(order[:-1], planned):
        place = z + sign * step

        def relay(m, place=place, sign=sign):
            for p in range(parts):
                own[p][place, m] = low(ready(p, place, m))
            if sign > 0:
                @pl.when(z > 0)
                def _():
                    for p in range(parts):
                        up_copy(p, place, m).wait_recv()
                        own[p][place, m] = low(wide(own[p][place, m]) + wide(below[p][place, m]))
            else:
                @pl.when(z < LINE - 1)
                def _():
                    for p in range(parts):
                        down_copy(p, place, m).wait_recv()
                        own[p][place, m] = low(wide(own[p][place, m]) + wide(above[p][place, m]))
            for p in range(parts):
                (up_copy if sign > 0 else down_copy)(p, place, m).start()

        under(okay, lambda relay=relay: each(relay))
        for d in hidden_now:
            over_plane(d)

    def settle(m):
        for p in range(parts):
            own[p][z, m] = low(ready(p, z, m))

        @pl.when(z > 0)
        def _():
            for p in range(parts):
                up_copy(p, z, m).wait_recv()
                own[p][z, m] = low(wide(own[p][z, m]) + wide(below[p][z, m]))

        @pl.when(z < LINE - 1)
        def _():
            for p in range(parts):
                down_copy(p, z, m).wait_recv()
                own[p][z, m] = low(wide(own[p][z, m]) + wide(above[p][z, m]))

    each(settle)
    for p in range(parts):
        kept.append(pltpu.make_async_copy(own[p].at[z, me], heads[p].at[me], local_sem.at[count + p]))
        kept[-1].start()
        for d, device in group.items():
            post.send(own[p].at[z, member(d)], heads[p].at[me], device, ("group", p, d))
    for p in range(parts):
        for d in GROUP[1:]:
            post.arrive(heads[p].at[member(d)], core_peer, ("group", p, d))
    for m in range(count):
        for d in PLANE:
            y_from, z_from = owner(d)
            post.arrive(landing(m, z_from * 2 + y_from), core_peer, ("plane", m, d))
    for sign, step, okay in order:
        place = z + sign * step

        def drain(m, place=place, sign=sign):
            for p in range(parts):
                to_row_copy(p, place, m).wait_send()
                if sign > 0:
                    up_copy(p, place, m).wait_send()
                if sign < 0:
                    down_copy(p, place, m).wait_send()

        under(okay, lambda drain=drain: each(drain))
    post.finish()
    for copy in kept:
        copy.wait()


def scatter_weights(head_sums, hidden_sums):
    parts, count = len(head_sums), len(hidden_sums)
    rows = head_sums[0].shape[0] // (2 * LINE * 4)
    width = hidden_sums[0].shape[1]
    anywhere = pl.BlockSpec(memory_space=pl.ANY)
    copies = (32 + 8 + 7) * count + 3 * parts
    outs = [jax.ShapeDtypeStruct((4, rows, h.shape[1]), jnp.bfloat16) for h in head_sums]
    outs += [jax.ShapeDtypeStruct((rows, LINE * 2 * width), jnp.bfloat16)] * count
    found = pl.pallas_call(
        functools.partial(scatter_kernel, parts, count),
        out_shape=outs,
        in_specs=[anywhere] * (parts + count),
        out_specs=[anywhere] * (parts + count),
        scratch_shapes=[
            pltpu.VMEM((LINE, 4, rows, h.shape[1]), jnp.bfloat16) for _ in range(4) for h in head_sums
        ]
        + [
            pltpu.VMEM((count, 2, LINE, 2, rows, width), jnp.bfloat16),
            pltpu.VMEM((count, 2, LINE, 2, rows, width), jnp.bfloat16),
            pltpu.VMEM((count, 2, LINE, rows, width), jnp.bfloat16),
            pltpu.SemaphoreType.DMA((copies,)),
            pltpu.SemaphoreType.DMA((copies,)),
            pltpu.SemaphoreType.DMA((parts, LINE, 4)),
            pltpu.SemaphoreType.DMA((parts, 3, LINE, 4)),
            pltpu.SemaphoreType.DMA((parts, 3, LINE, 4)),
            pltpu.SemaphoreType.DMA((count + parts + 16 * count,)),
        ],
        compiler_params=pltpu.CompilerParams(
            collective_id=1, has_side_effects=True, vmem_limit_bytes=56 << 20
        ),
    )(
        *[h.reshape(2, LINE, 4, rows, h.shape[1]) for h in head_sums],
        *[h.reshape(2, LINE, 2, 2, rows, width) for h in hidden_sums],
    )
    return found[:parts], found[parts:]


def split_columns(matrix, count):
    rows, cols = matrix.shape
    return matrix.reshape(rows, count, cols // count).transpose(1, 0, 2)


def join_columns(blocks):
    count, rows, cols = blocks.shape
    return wide(blocks).transpose(1, 0, 2).reshape(rows, count * cols)


def turn(values, cosine, sine):
    half_dim = HEAD_DIM // 2
    front_half = values[..., :half_dim]
    back_half = values[..., half_dim:]
    return jnp.concatenate(
        [front_half * cosine - back_half * sine, back_half * cosine + front_half * sine], axis=-1
    )


def dot(left_side, right_side):
    return jnp.dot(left_side, right_side, preferred_element_type=jnp.float32)


def dot_rows(left_side, right_side):
    return jnp.einsum("tf,df->td", left_side, right_side, preferred_element_type=jnp.float32)


def outer_sum(left_side, right_side):
    return jnp.einsum("td,tf->df", left_side, right_side, preferred_element_type=jnp.float32)


def per_device_line(
    tokens,
    cotangent,
    doc_ids,
    bit_levels,
    w_query,
    w_key,
    w_value,
    w_proj,
    w_gate,
    w_up,
    w_down,
    gain_first,
    gain_second,
    gain_third,
    gain_fourth,
):
    spot = Spot()
    count = tokens.shape[1]
    group_size = HEADS // KV_HEADS
    query_width = HEADS * HEAD_DIM
    score_scale = HEAD_DIM ** (-0.5)
    span = 4 * count

    heads_in = low(
        jnp.concatenate(
            [
                split_columns(dequant(w_query, bit_levels[0], D, qk_boost), KV_HEADS),
                split_columns(dequant(w_key, bit_levels[1], D, qk_boost), KV_HEADS),
                split_columns(dequant(w_value, bit_levels[2], D, 1.0), KV_HEADS),
                split_columns(dequant(w_proj, bit_levels[3], query_width, 1.0), KV_HEADS),
            ],
            axis=2,
        )
    )
    flat_tokens = wide(tokens).reshape(count, D)
    normed_low = low(rmsnorm(flat_tokens, gain_first))
    all_heads, normed_all, (gate_w, up_w, down_w) = gather_weights(
        heads_in,
        normed_low,
        [
            low(dequant(w_gate, bit_levels[4], D, 1.0)),
            low(dequant(w_up, bit_levels[5], D, 1.0)),
            low(dequant(w_down, bit_levels[6], FF, 1.0)),
        ],
    )
    head_width = (group_size + 2) * HEAD_DIM
    heads_w = all_heads[:, :head_width]
    proj_w = all_heads[:, head_width:]

    inner = jnp.arange(count, dtype=jnp.int32)
    offsets = jnp.concatenate(
        [member(spot, dx, dc) * count + inner for dx in range(2) for dc in range(2)]
    )
    positions = spot.z * span + offsets
    half_dim = HEAD_DIM // 2
    frequency = 10000.0 ** (-(2.0 / HEAD_DIM) * jnp.arange(half_dim, dtype=jnp.float32))
    angles = positions.astype(jnp.float32)[:, None] * frequency[None, :]
    cosine = jnp.cos(angles)
    sine = jnp.sin(angles)
    docs = doc_ids.reshape(LINE, 2, 2, count)
    docs = jnp.where(spot.x == 1, docs[:, ::-1], docs)
    docs = jnp.where(spot.c == 1, docs[:, :, ::-1], docs).reshape(LINE, span)
    query_docs = pick(docs, spot.z)

    pre = dot(normed_all, heads_w)
    wide_q = group_size * HEAD_DIM
    query_rot = low(
        turn(
            pre[:, :wide_q].reshape(span, group_size, HEAD_DIM),
            cosine[:, None],
            sine[:, None],
        )
    )
    key_rot = low(turn(pre[:, wide_q : wide_q + HEAD_DIM], cosine, sine))
    value_low = low(pre[:, wide_q + HEAD_DIM :])
    key_value = [jnp.concatenate([key_rot, value_low], axis=1)]
    for _ in range(1, LINE):
        key_value.append(up_line(key_value[-1]))

    totals = 0.0
    summed = 0.0
    saved = []
    for back, block in enumerate(key_value):
        key_piece, value_piece = block[:, :HEAD_DIM], block[:, HEAD_DIM:]
        key_docs = pick(docs, jnp.maximum(spot.z - back, 0))
        key_pos = positions - back * span
        allowed = (
            (key_pos[None, :] <= positions[:, None])
            & (key_pos[None, :] >= 0)
            & (key_docs[None, :] == query_docs[:, None])
        )
        raw_scores = (
            jnp.einsum("qrd,kd->rqk", query_rot, key_piece, preferred_element_type=jnp.float32)
            * score_scale
        )
        bent = jnp.tanh(raw_scores / softcap)
        weights = jnp.where(allowed[None], jnp.exp(softcap * bent), 0.0)
        totals = totals + jnp.sum(weights, axis=-1)
        summed = summed + jnp.einsum(
            "rqk,kd->qrd", low(weights), value_piece, preferred_element_type=jnp.float32
        )
        saved.append((key_piece, value_piece, weights, bent))
    denominator = jnp.transpose(totals)[..., None]
    mixed_out = summed / denominator
    mixed_low = low(mixed_out).reshape(span, wide_q)
    attn_out = reduce_group(low(dot_rows(mixed_low, proj_w)).reshape(2, 2, count, D))
    hidden_one = flat_tokens + rmsnorm(attn_out, gain_second)
    mid_low = low(rmsnorm(hidden_one, gain_third))

    mid_chunks = gather_plane(spot, mid_low)
    gates, acts, ffn_chunks = [], [], []
    for chunk in mid_chunks:
        gate_pre = dot(chunk, gate_w)
        up_pre = dot(chunk, up_w)
        activated = low(gelu_product(gate_pre, up_pre))
        gates.append((gate_pre, up_pre))
        acts.append(activated)
        ffn_chunks.append(low(dot_rows(activated, down_w)).reshape(2, count, D))
    ffn_out = reduce_plane(lax.optimization_barrier(ffn_chunks))
    result = hidden_one + rmsnorm(ffn_out, gain_fourth)
    layer_out = low(result).reshape(1, count, D)

    upstream = wide(cotangent).reshape(count, D)
    grad_ffn, fourth_part = jax.vjp(rmsnorm, ffn_out, gain_fourth)[1](upstream)
    grad_chunks = gather_plane(spot, low(grad_ffn))
    gate_grads, up_grads, back_chunks = [], [], []
    for chunk, (gate_pre, up_pre) in zip(grad_chunks, gates):
        grad_act = dot(chunk, down_w)
        grad_gate_pre, grad_up_pre = jax.vjp(gelu_product, gate_pre, up_pre)[1](grad_act)
        gate_grads.append(low(grad_gate_pre))
        up_grads.append(low(grad_up_pre))
        back_chunks.append(
            low(dot_rows(gate_grads[-1], gate_w) + dot_rows(up_grads[-1], up_w)).reshape(
                2, count, D
            )
        )
    grad_mid = reduce_plane(lax.optimization_barrier(back_chunks))
    grad_mid, mid_chunks, gate_grads, up_grads, grad_chunks, acts = lax.optimization_barrier(
        (grad_mid, mid_chunks, gate_grads, up_grads, grad_chunks, acts)
    )
    mid_all = jnp.concatenate(mid_chunks, axis=0)
    gate_sums = low(outer_sum(mid_all, jnp.concatenate(gate_grads, axis=0)))
    up_sums = low(outer_sum(mid_all, jnp.concatenate(up_grads, axis=0)))
    down_sums = low(
        outer_sum(jnp.concatenate(grad_chunks, axis=0), jnp.concatenate(acts, axis=0))
    )

    hidden_part, third_part = jax.vjp(rmsnorm, hidden_one, gain_third)[1](grad_mid)
    grad_hidden = upstream + hidden_part
    grad_attn, second_part = jax.vjp(rmsnorm, attn_out, gain_second)[1](grad_hidden)
    grad_attn_all = gather_group(low(grad_attn))
    proj_sums = low(outer_sum(grad_attn_all, mixed_low))

    grad_mixed = dot(grad_attn_all, proj_w).reshape(span, group_size, HEAD_DIM)
    grad_summed = low(grad_mixed / denominator)
    delta = jnp.transpose(jnp.sum(grad_mixed * mixed_out, axis=-1)) / totals
    grad_query_rot = 0.0
    passed = None
    for back in range(LINE - 1, -1, -1):
        key_piece, value_piece, weights, bent = saved[back]
        grad_weights = (
            jnp.einsum(
                "qrd,kd->rqk", grad_summed, value_piece, preferred_element_type=jnp.float32
            )
            - delta[..., None]
        )
        grad_raw = low(weights * grad_weights * (1.0 - bent * bent))
        grad_query_rot = grad_query_rot + jnp.einsum(
            "rqk,kd->qrd", grad_raw, key_piece, preferred_element_type=jnp.float32
        )
        key_term = (
            jnp.einsum("rqk,qrd->kd", grad_raw, query_rot, preferred_element_type=jnp.float32)
            * score_scale
        )
        value_term = jnp.einsum(
            "rqk,qrd->kd", low(weights), grad_summed, preferred_element_type=jnp.float32
        )
        sums = jnp.concatenate([key_term, value_term], axis=1)
        if passed is not None:
            sums = sums + wide(down_line(passed))
        passed = low(sums)
    grad_query_pre = low(
        turn(grad_query_rot * score_scale, cosine[:, None], -sine[:, None])
    ).reshape(span, wide_q)
    grad_key_pre = low(turn(sums[:, :HEAD_DIM], cosine, -sine))
    grad_pre = jnp.concatenate([grad_query_pre, grad_key_pre, low(sums[:, HEAD_DIM:])], axis=1)
    grad_shares = dot_rows(grad_pre, heads_w)
    first_part = jnp.sum(wide(normed_all) * grad_shares, axis=0) / (1.0 + gain_first)
    gain_sums = jnp.stack([first_part, second_part, third_part, fourth_part], axis=1)
    gain_sums = low(jnp.pad(gain_sums, ((0, 0), (0, 124))))
    (head_rows, proj_rows), (grad_gate, grad_up, grad_down) = scatter_weights(
        [
            low(outer_sum(normed_all, grad_pre)),
            jnp.concatenate([proj_sums, gain_sums], axis=1),
        ],
        [gate_sums, up_sums, down_sums],
    )
    grad_in = reduce_group(low(grad_shares).reshape(2, 2, count, D))
    tokens_part = jax.vjp(lambda v: rmsnorm(v, gain_first), flat_tokens)[1](grad_in)[0]
    grad_tokens = (grad_hidden + tokens_part).reshape(1, count, D)
    gains = jnp.sum(wide(proj_rows[:, :, wide_q:]), axis=0)
    return (
        layer_out,
        grad_tokens,
        join_columns(head_rows[:, :, :wide_q]),
        join_columns(head_rows[:, :, wide_q : wide_q + HEAD_DIM]),
        join_columns(head_rows[:, :, wide_q + HEAD_DIM :]),
        join_columns(proj_rows[:, :, :wide_q]),
        wide(grad_gate),
        wide(grad_up),
        wide(grad_down),
        gains[:, 0],
        gains[:, 1],
        gains[:, 2],
        gains[:, 3],
    )


def solution(mesh):
    placed = (
        P("rows", "seq", None),
        P("rows", "seq", None),
        P("rows", None),
        P(),
        P(("rows", "seq"), None),
        P(("rows", "seq"), None),
        P(("rows", "seq"), None),
        P(("rows", "seq"), None),
        P(("rows", "seq"), None),
        P(("rows", "seq"), None),
        P(("rows", "seq"), None),
        P(),
        P(),
        P(),
        P(),
    )
    sizes = dict(mesh.shape)
    fits = sizes["rows"] == 2 and sizes["seq"] == LINE * 4
    return jax.shard_map(
        per_device_line if fits else per_device_plain,
        mesh=mesh,
        in_specs=placed,
        out_specs=(
            P("rows", "seq", None),
            P("rows", "seq", None),
            P(("rows", "seq"), None),
            P(("rows", "seq"), None),
            P(("rows", "seq"), None),
            P(("rows", "seq"), None),
            P(("rows", "seq"), None),
            P(("rows", "seq"), None),
            P(("rows", "seq"), None),
            P(("rows", "seq")),
            P(("rows", "seq")),
            P(("rows", "seq")),
            P(("rows", "seq")),
        ),
        check_vma=False,
    )
```
